256 devices in a mesh: dp: 16 (over z_hi, y), sub: 16 (over x, z_lo, core).
Axes of the slice: x: 4, y: 4, z: 8 (z_hi: 4, z_lo: 2; z = z_hi * 2 + z_lo), core: 2. Of those that a mesh axis runs over, the one named last changes fastest.
Arguments:
- vectors: bfloat16 [32768, 2048], P(('dp', 'sub')), may hold values from -24 to 24
- rotation: bfloat16 [2048, 2048], P(None, 'sub'), may hold values from -0.125 to 0.125
- codebook: bfloat16 [16, 4096, 128], P('sub'), may hold values from -6 to 6
- codes: int32 [32768, 16], P('dp', 'sub'), may hold values from 0 to 4095
Outputs:
- centroids: bfloat16 [16, 4096, 128], P('sub')
- distortion: float32 [32768, 16], P('dp', 'sub')
- cross: float32 [2048, 2048], P('dp', 'sub')
The draws below stay inside these ranges and needn't reach their ends.
All inputs are finite; a program needn't handle non-finite values.
Results may differ from the reference program's by a relative error of at most 0.0047.
Values may be sent and summed in bfloat16 or wider, within the bound.
A program may use at most 64 MiB of HBM per device.

```python
import jax
import jax.numpy as jnp
from jax import lax

D = 2048
M = 16
K = 4096
DS = 128
ROWS = 32768


def set_ends(array, own_key, smallest, largest):
    extent = array.shape
    place = [jax.random.randint(jax.random.fold_in(own_key, axis), (), 0, extent[axis]) for axis in range(len(extent))]
    array = array.at[tuple(place)].set(smallest)
    longest = extent.index(max(extent))
    place[longest] = (place[longest] + 1) % extent[longest]
    return array.at[tuple(place)].set(largest)


def spiked(result, key, source, target, shards_of, factor):
    def block_of(dim):
        return (jnp.arange(result.shape[dim]) // (result.shape[dim] // shards_of)).reshape((-1,) + (1,) * (result.ndim - 1 - dim))

    near = jax.random.permutation(key, shards_of)[block_of(target)]
    far = (block_of(target) + shards_of // 2) % shards_of
    return jnp.where((block_of(source) == near) | (block_of(source) == far), factor * result, result)


def block_levels(key, dims, split, low, top_value):
    factor_of, own = 1.0, jax.random.fold_in(key, 6)
    for axis_at, shards_of in split:
        draws = jnp.exp(jax.random.uniform(jax.random.fold_in(own, axis_at), (shards_of,), jnp.float32, low / len(split), top_value / len(split)))
        factor_of = factor_of * jnp.repeat(draws, dims[axis_at] // shards_of).reshape([-1 if axis == axis_at else 1 for axis in range(len(dims))])
    return factor_of


def gaussian(rng, extent, deviation, reach, cuts=(), kind=jnp.bfloat16):
    drawn = jax.random.normal(rng, extent, jnp.float32) * deviation
    if len(cuts) > 0:
        drawn = block_levels(rng, extent, cuts, -0.22, 0.18) * drawn
    return jnp.clip(drawn, min=-reach, max=reach).astype(kind)


def heavy_noise(key, dims, deviation, bound, cuts, heavy, kind=jnp.bfloat16):
    array = deviation * jax.random.normal(key, dims, jnp.float32)
    if cuts:
        array = array * block_levels(key, dims, cuts, -0.22, 0.18)
    return jnp.clip(spiked(array, jax.random.fold_in(key, 3), *heavy), -bound, bound).astype(kind)


def setup_inputs(seed: int = 0) -> dict:
    seeds = jax.random.split(jax.random.key(seed), 5)
    return {
        "vectors": heavy_noise(seeds[0], (ROWS, D), 1.0, 24.0, ((0, 256),), (0, 1, 256, 6.0)),
        "rotation": gaussian(seeds[1], (D, D), D ** -0.5, 0.125, ((1, 16),)),
        "codebook": gaussian(seeds[2], (M, K, DS), 1.0, 6.0, ((0, 16),)),
        "codes": set_ends(jax.random.randint(seeds[3], (ROWS, M), 0, K), jax.random.fold_in(seeds[3], 1), 0, K - 1).astype(jnp.int32),
    }


def one_subspace(operands):
    values, labels, codewords = operands
    count = codewords.shape[0]
    totals = jax.ops.segment_sum(values.astype(jnp.float32), labels, num_segments=count)
    members = jax.ops.segment_sum(jnp.ones(labels.shape, jnp.float32), labels, num_segments=count)
    centroid = ((totals + codewords.astype(jnp.float32)) / (members[:, None] + 1.0)).astype(jnp.bfloat16)
    rebuilt = jnp.take(centroid, labels, axis=0)
    distance = jnp.sum((values.astype(jnp.float32) - rebuilt.astype(jnp.float32)) ** 2, axis=-1)
    return centroid, rebuilt, distance


def reference(vectors, rotation, codebook, codes):
    total_rows = vectors.shape[0]
    rotated = jnp.dot(vectors, rotation, preferred_element_type=jnp.float32).astype(jnp.bfloat16)
    pieces = rotated.reshape(total_rows, M, DS).transpose(1, 0, 2)
    centroid, rebuilt, distance = lax.map(one_subspace, (pieces, codes.T.astype(jnp.int32), codebook))
    rebuilt_rows = rebuilt.transpose(1, 0, 2).reshape(total_rows, D)
    cross = lax.dot_general(vectors, rebuilt_rows, (((0,), (0,)), ((), ())), preferred_element_type=jnp.float32)
    return centroid, distance.T, cross
```

```python
import jax
import jax.numpy as jnp
from jax import lax
from jax.experimental import pallas as pl
from jax.experimental.pallas import tpu as pltpu
from jax.sharding import PartitionSpec as P

BF16 = jnp.bfloat16
F32 = jnp.float32
MESH = pl.DeviceIdType.MESH

D = 2048
K = 4096
DS = 128
GROUP = 2048
OWN = 256
SEMS = 160


def kernel(
    v_ref, r_ref, cb_ref, codes_ref,
    cent_out, dist_ref, cross_ref,
    vg, rot, oth, rott, rown, roth, raw, codes, lo, hicol, counts, tacc, tsend, trecv, cnt, cbk, cent,
    reb, rebb, xf, xs, xr, zs, zr,
    ssem, rsem, lsem,
):
    dp = lax.axis_index("dp")
    sub = lax.axis_index("sub")
    zh, y = lax.div(dp, 4), lax.rem(dp, 4)
    x, zl, core = lax.div(sub, 4), lax.rem(lax.div(sub, 2), 2), lax.rem(sub, 2)
    xp, xm, x2 = lax.rem(x + 1, 4), lax.rem(x + 3, 4), lax.rem(x + 2, 4)
    yp, ym, y2 = lax.rem(y + 1, 4), lax.rem(y + 3, 4), lax.rem(y + 2, 4)
    zo, co = 1 - zl, 1 - core

    def sid(a, b, c):
        return a * 4 + b * 2 + c

    to_xp, to_xm = (dp, sid(xp, zl, core)), (dp, sid(xm, zl, core))
    to_z = (dp, sid(x, zo, core))
    to_core = (dp, sid(x, zl, co))
    to_out = (lax.rem(zh + 3 + 2 * zl, 4) * 4 + y, sid(x, zo, core))

    def to_y(k):
        return (zh * 4 + lax.rem(y + k, 4), sub)

    def to_zh(k):
        return (lax.rem(zh + k, 4) * 4 + y, sub)

    pending = []
    ids = {}

    def role(name):
        return ids.setdefault(name, len(ids))

    def send(name, src, dst, target):
        i = role(name)
        copy = pltpu.make_async_remote_copy(
            src_ref=src, dst_ref=dst, send_sem=ssem.at[i], recv_sem=rsem.at[i],
            device_id=target, device_id_type=MESH,
        )
        copy.start()
        pending.append(copy)

    def recv(name, ref):
        i = role(name)
        pltpu.make_async_remote_copy(
            src_ref=ref, dst_ref=ref, send_sem=ssem.at[i], recv_sem=rsem.at[i],
            device_id=to_core, device_id_type=MESH,
        ).wait_recv()

    def piece(cp, h, c):
        return pl.ds(pl.multiple_of(cp * 256 + h * 128 + c * 64, 64), 64)

    def unit(cp, h):
        return pl.ds(pl.multiple_of(cp * 256 + h * 128, 128), 128)

    def chip(cp):
        return pl.ds(pl.multiple_of(cp * 256, 256), 256)

    here, up, down, far = x * 2 + zl, xp * 2 + zl, xm * 2 + zl, x2 * 2 + zl
    here_z, up_z, down_z, far_z = x * 2 + zo, xp * 2 + zo, xm * 2 + zo, x2 * 2 + zo

    local = [
        pltpu.make_async_copy(v_ref.at[pl.ds(h * 64, 64)], vg.at[piece(here, h, core)], lsem.at[h])
        for h in range(2)
    ]
    local.append(pltpu.make_async_copy(codes_ref, raw, lsem.at[2]))
    local.append(pltpu.make_async_copy(r_ref, rown, lsem.at[3]))
    hi_own = 4 * y + zh
    own_rows = pl.ds(pl.multiple_of(hi_own * OWN, OWN), OWN)
    local.append(pltpu.make_async_copy(cb_ref.at[own_rows], cbk, lsem.at[4]))
    for copy in local:
        copy.start()

    barrier = pltpu.get_barrier_semaphore()
    peers = [to_xp, to_xm, to_z, to_core, to_out] + [to_y(k) for k in (1, 3, 2)] + [to_zh(k) for k in (1, 3, 2)]
    for peer in peers:
        pl.semaphore_signal(barrier, inc=1, device_id=peer, device_id_type=MESH)
    for copy in local:
        copy.wait()

    even, odd = raw[pl.ds(0, 8, stride=2), :], raw[pl.ds(1, 8, stride=2), :]
    first = lax.broadcasted_iota(jnp.int32, (8, 128), 1) < 64
    codes[y, 0:8, :] = jnp.where(first, even, pltpu.roll(odd, 64, 1))
    codes[y, 8:16, :] = jnp.where(first, pltpu.roll(even, 64, 1), odd)
    pl.semaphore_wait(barrier, len(peers))

    def vsend(name, cp, h, c, target):
        ref = vg.at[piece(cp, h, c)]
        send(name, ref, ref, target)

    def vrecv(name, cp, h, c):
        recv(name, vg.at[piece(cp, h, c)])

    vsend("xm0", here, 0, core, to_xp)
    vsend("xp1", here, 1, core, to_xm)
    top, low = pl.ds(0, 1024), pl.ds(1024, 1024)
    send("r_in", rown.at[top], roth.at[top], to_z)
    send("r_out", rown.at[low], roth.at[low], to_out)
    for h in range(2):
        vsend("d_own%d" % h, here, h, core, to_core)
    for k in (1, 3, 2):
        send("code%d" % k, codes.at[y], codes.at[y], to_y(k))
    vsend("xm1", here, 1, core, to_xp)
    vsend("xp0", here, 0, core, to_xm)

    def y_send(name, rows, direct):
        ref = rot.at[y, rows]
        send("a" + name, ref, ref, to_y(1))
        send("b" + name, ref, ref, to_y(3))
        if direct:
            send("c" + name, ref, ref, to_y(2))

    def halves(start, size):
        a = pl.ds(pl.multiple_of(start, 64), size)
        b = pl.ds(pl.multiple_of(start + size, 64), size)
        return a, b

    def y_forward(name, start, size):
        rows = pl.ds(pl.multiple_of(start, 128), size)
        a, b = halves(start, size // 2)
        recv("a" + name, rot.at[ym, rows])
        ref = rot.at[ym, a]
        send("c" + name, ref, ref, to_y(1))
        recv("b" + name, rot.at[yp, rows])
        ref = rot.at[yp, b]
        send("d" + name, ref, ref, to_y(3))

    def y_last(name, start, size, direct):
        if direct:
            rows = pl.ds(pl.multiple_of(start, 128), size)
            recv("a" + name, rot.at[ym, rows])
            recv("b" + name, rot.at[yp, rows])
            recv("c" + name, rot.at[y2, rows])
        else:
            a, b = halves(start, size // 2)
            recv("c" + name, rot.at[y2, a])
            recv("d" + name, rot.at[y2, b])

    def rot_own(rows):
        part = jnp.dot(vg[rows, :], rown[...], preferred_element_type=F32)
        rot[y, rows, :] = part.astype(BF16)

    def rot_oth(rows):
        part = jnp.dot(vg[rows, :], roth[...], preferred_element_type=F32)
        oth[rows, :] = part.astype(BF16)

    def rot_both(rows):
        both = jnp.concatenate([rown[...], roth[...]], axis=1)
        part = jnp.dot(vg[rows, :], both, preferred_element_type=F32)
        rot[y, rows, :] = part[:, :DS].astype(BF16)
        oth[rows, :] = part[:, DS:].astype(BF16)

    def z_send(name, rows):
        send("z" + name, oth.at[rows], rot.at[y, rows], to_z)

    def z_recv(name, rows):
        recv("z" + name, rot.at[y, rows])

    for h in range(2):
        vrecv("d_own%d" % h, here, h, co)
    rot_own(chip(here))
    y_send("A", chip(here), False)

    for k in (1, 3, 2):
        recv("code%d" % k, codes.at[lax.rem(y + 4 - k, 4)])
    tacc[...] = jnp.zeros_like(tacc)
    iota = lax.broadcasted_iota(jnp.int32, (256, 128), 0)

    def lo_table(g, carry):
        tile = jnp.bitwise_and(codes[g], 255)
        for i in range(16):
            cp, h = i // 2, i % 2
            row = tile[h * 8 + cp:h * 8 + cp + 1, :]
            mark = jnp.where(iota == jnp.broadcast_to(row, (256, 128)), 1.0, 0.0)
            lo[:, pl.ds(pl.multiple_of(g * GROUP + i * 128, 128), 128)] = mark.astype(BF16)
        return carry

    lax.fori_loop(0, 4, lo_table, 0)

    def hi_table(g, carry):
        tile = lax.shift_right_logical(codes[g], 8).astype(F32)
        for i in range(16):
            cp, h = i // 2, i % 2
            row = tile[h * 8 + cp:h * 8 + cp + 1, :]
            hicol[g, i * 128:(i + 1) * 128, :] = jnp.broadcast_to(row, (128, 128)).T.astype(BF16)
        return carry

    vrecv("xm0", down, 0, core)
    vsend("x20", down, 0, core, to_xp)
    vsend("d_xm0", down, 0, core, to_core)
    vrecv("xp1", up, 1, core)
    vsend("x21", up, 1, core, to_xm)
    vsend("d_xp1", up, 1, core, to_core)
    recv("r_in", roth.at[top])
    recv("r_out", roth.at[low])
    rot_oth(chip(here))
    z_send("A", chip(here))
    vrecv("d_xm0", down, 0, co)
    rot_both(unit(down, 0))
    y_send("B", unit(down, 0), False)
    z_send("B", unit(down, 0))
    vrecv("d_xp1", up, 1, co)
    rot_both(unit(up, 1))
    y_send("C", unit(up, 1), False)
    z_send("C", unit(up, 1))
    vsend("w0", here, 0, core, to_z)
    y_forward("A", here * 256, 256)
    lax.fori_loop(0, 4, hi_table, 0)

    z_recv("A", chip(here_z))
    y_send("Az", chip(here_z), False)
    z_recv("B", unit(down_z, 0))
    y_send("Bz", unit(down_z, 0), False)
    z_recv("C", unit(up_z, 1))
    y_send("Cz", unit(up_z, 1), False)
    y_forward("B", down * 256, 128)
    y_forward("C", up * 256 + 128, 128)

    def count(g, acc):
        for h in range(2):
            for cp in range(8):
                row = lax.shift_right_logical(codes[g, h * 8 + cp:h * 8 + cp + 1, :], 8)
                mark = jnp.where(iota[:16] == jnp.broadcast_to(row, (16, 128)), 1.0, 0.0).astype(BF16)
                tab = lo[:, pl.ds(pl.multiple_of(g * GROUP + (cp * 2 + h) * 128, 128), 128)]
                acc = acc + lax.dot_general(mark, tab, (((1,), (1,)), ((), ())), preferred_element_type=F32)
        return acc

    counts[0] = lax.fori_loop(0, 4, count, jnp.zeros((16, 256), F32))
    for k in (1, 3, 2):
        send("n%d" % k, counts.at[0], counts.at[k], to_zh(k))

    vrecv("xm1", down, 1, core)
    vsend("d_xm1", down, 1, core, to_core)
    vrecv("xp0", up, 0, core)
    vsend("d_xp0", up, 0, core, to_core)
    vrecv("d_xm1", down, 1, co)
    rot_both(unit(down, 1))
    y_send("D", unit(down, 1), False)
    z_send("D", unit(down, 1))
    vrecv("d_xp0", up, 0, co)
    rot_both(unit(up, 0))
    y_send("E", unit(up, 0), False)
    z_send("E", unit(up, 0))
    vsend("w1", here, 1, core, to_z)
    y_forward("Az", here_z * 256, 256)
    y_forward("Bz", down_z * 256, 128)
    y_forward("Cz", up_z * 256 + 128, 128)

    def accumulate(cp):
        def body(g, carry):
            marks = lo[:, pl.ds(pl.multiple_of(g * GROUP + cp * 256, 256), 256)]
            values = rot[g, chip(cp), :]
            his = hicol[g, chip(cp), :]
            parts = []
            for h in range(4):
                want = (4 * y + h).astype(F32).astype(BF16)
                parts.append(jnp.where(his == want, values, jnp.zeros_like(values)))
            wide = jnp.concatenate(parts, axis=1)
            tacc[...] += jnp.dot(marks, wide, preferred_element_type=F32)
            return carry

        lax.fori_loop(0, 4, body, 0)

    y_last("A", here * 256, 256, False)
    accumulate(here)
    z_recv("D", unit(down_z, 1))
    y_send("Dz", unit(down_z, 1), False)
    z_recv("E", unit(up_z, 0))
    y_send("Ez", unit(up_z, 0), False)
    y_forward("D", down * 256 + 128, 128)
    y_forward("E", up * 256, 128)
    y_last("Az", here_z * 256, 256, False)
    accumulate(here_z)

    vrecv("x20", far, 0, core)
    vsend("d_x20", far, 0, core, to_core)
    vrecv("x21", far, 1, core)
    vsend("d_x21", far, 1, core, to_core)
    for h in range(2):
        vrecv("d_x2%d" % h, far, h, co)
    rot_both(chip(far))
    z_send("F", chip(far))
    y_send("F", chip(far), True)
    y_forward("Dz", down_z * 256 + 128, 128)
    y_forward("Ez", up_z * 256, 128)

    vrecv("w0", here_z, 0, core)
    vsend("wm0", here_z, 0, core, to_xp)
    vsend("wp0", here_z, 0, core, to_xm)
    vsend("d_w0", here_z, 0, core, to_core)
    z_recv("F", chip(far_z))
    y_send("Fz", chip(far_z), True)
    y_last("B", down * 256, 128, False)
    y_last("D", down * 256 + 128, 128, False)
    accumulate(down)
    y_last("C", up * 256 + 128, 128, False)
    y_last("E", up * 256, 128, False)
    accumulate(up)
    vrecv("w1", here_z, 1, core)
    vsend("wp1", here_z, 1, core, to_xm)
    vsend("wm1", here_z, 1, core, to_xp)
    vsend("d_w1", here_z, 1, core, to_core)
    y_last("Bz", down_z * 256, 128, False)
    y_last("Dz", down_z * 256 + 128, 128, False)
    accumulate(down_z)
    y_last("Cz", up_z * 256 + 128, 128, False)
    y_last("Ez", up_z * 256, 128, False)
    accumulate(up_z)
    y_last("F", far * 256, 256, True)
    accumulate(far)
    y_last("Fz", far_z * 256, 256, True)
    accumulate(far_z)

    for k in (2, 1, 3):
        theirs = pl.ds(pl.multiple_of(lax.rem(zh + k, 4) * DS, DS), DS)
        tsend[k - 1] = tacc[:, theirs].astype(BF16)
        send("t%d" % k, tsend.at[k - 1], trecv.at[k - 1], to_zh(k))
    for k in (1, 3, 2):
        recv("n%d" % k, counts.at[k])
    number = counts[0] + counts[1] + counts[2] + counts[3]
    counts[4] = number
    mine = counts[4, pl.ds(hi_own, 1), :]
    cnt[...] = jnp.broadcast_to(mine, (128, 256)).T
    rott[...] = rot[y].astype(F32).T
    vrecv("wm0", down_z, 0, core)
    vsend("w20", down_z, 0, core, to_xp)
    vsend("d_wm0", down_z, 0, core, to_core)
    vrecv("wp1", up_z, 1, core)
    vsend("w21", up_z, 1, core, to_xm)
    vsend("d_wp1", up_z, 1, core, to_core)
    total = tacc[:, pl.ds(pl.multiple_of(zh * DS, DS), DS)]
    for k in (1, 3, 2):
        recv("t%d" % k, trecv.at[k - 1])
        total = total + trecv[k - 1].astype(F32)
    cent[own_rows, :] = ((total + cbk[...].astype(F32)) / (cnt[...] + 1.0)).astype(BF16)

    def chunk(a, b):
        return pl.ds(pl.multiple_of(b * 1024 + a * OWN, OWN), OWN)

    def half_chunk(a, b, h):
        return pl.ds(pl.multiple_of(b * 1024 + a * OWN + h * 128, 128), 128)

    outs = []

    def rebuild(a, b):
        copy = pltpu.make_async_copy(
            cent.at[chunk(a, b)], cent_out.at[chunk(a, b)], lsem.at[5 + len(outs)]
        )
        copy.start()
        outs.append(copy)
        table = cent[chunk(a, b), :].astype(F32).T.astype(BF16)
        want = 4 * b + a

        def body(i, carry):
            tab = lo[:, pl.ds(pl.multiple_of(y * GROUP + i * 256, 256), 256)]
            got = jnp.dot(table, tab, preferred_element_type=F32)
            place = pl.ds(pl.multiple_of(i * 256, 256), 256)
            row = jnp.concatenate([codes[y, pl.ds(i, 1), :], codes[y, pl.ds(i + 8, 1), :]], axis=1)
            hit = lax.shift_right_logical(row, 8) == want
            reb[:, place] = jnp.where(jnp.broadcast_to(hit, (128, 256)), got, reb[:, place])
            return carry

        lax.fori_loop(0, 8, body, 0)

    def y_chunk_send(q, a):
        ref = cent.at[chunk(a, y)]
        send("ca%d" % q, ref, ref, to_y(1))
        send("cb%d" % q, ref, ref, to_y(3))

    def y_chunk_forward(q, a):
        recv("ca%d" % q, cent.at[chunk(a, ym)])
        ref = cent.at[half_chunk(a, ym, 0)]
        send("cc%d" % q, ref, ref, to_y(1))
        recv("cb%d" % q, cent.at[chunk(a, yp)])
        ref = cent.at[half_chunk(a, yp, 1)]
        send("cd%d" % q, ref, ref, to_y(3))

    reb[...] = jnp.zeros_like(reb)
    zs_of = [zh] + [lax.rem(zh + 4 - q, 4) for q in (1, 2, 3)]
    for k in (2, 1, 3):
        ref = cent.at[own_rows]
        send("cz%d" % k, ref, ref, to_zh(k))
    y_chunk_send(0, zh)
    rebuild(zh, y)
    y_chunk_forward(0, zh)
    order = (1, 3, 2)
    before = 0
    for q in order:
        a = zs_of[q]
        recv("cz%d" % q, cent.at[chunk(a, y)])
        y_chunk_send(q, a)
        if before:
            y_chunk_forward(before, zs_of[before])
        rebuild(a, y)
        rebuild(zs_of[before], ym)
        rebuild(zs_of[before], yp)
        before = q
    y_chunk_forward(before, zs_of[before])
    for b in (ym, yp):
        rebuild(zs_of[before], b)

    vrecv("wm1", down_z, 1, core)
    vsend("d_wm1", down_z, 1, core, to_core)
    vrecv("wp0", up_z, 0, core)
    vsend("d_wp0", up_z, 0, core, to_core)
    vrecv("w20", far_z, 0, core)
    vsend("d_w20", far_z, 0, core, to_core)
    vrecv("w21", far_z, 1, core)
    vsend("d_w21", far_z, 1, core, to_core)
    for q in (0,) + order:
        a = zs_of[q]
        recv("cc%d" % q, cent.at[half_chunk(a, y2, 0)])
        recv("cd%d" % q, cent.at[half_chunk(a, y2, 1)])
        rebuild(a, y2)
    for h in range(2):
        vrecv("d_w%d" % h, here_z, h, co)
        vrecv("d_wm%d" % h, down_z, h, co)
        vrecv("d_wp%d" % h, up_z, h, co)
        vrecv("d_w2%d" % h, far_z, h, co)

    rebb[...] = reb[...].astype(BF16)

    def cross_half(p):
        def body(i, carry):
            place = pl.ds(pl.multiple_of(i * 512 + p * 256, 256), 256)
            part = jnp.dot(rebb[...], vg[:, place], preferred_element_type=F32)
            xf[2 * p, i] = part[:, :128]
            xf[2 * p + 1, i] = part[:, 128:]
            return carry

        lax.fori_loop(0, 4, body, 0)

    def cross_send(k):
        xs[k - 1] = xf[lax.rem(y + k, 4)].astype(BF16)
        send("xa%d" % k, xs.at[k - 1], xr.at[k - 1], to_y(k))

    near = lax.div(y, 2)
    cross_half(1 - near)
    cross_send(2)
    cross_half(near)
    cross_send(1)
    cross_send(3)

    gap = rott[...] - reb[...]
    gap = jnp.sum(gap * gap, axis=0, keepdims=True)
    half_row = lax.broadcasted_iota(jnp.int32, (1, 128), 1) < 64
    for cp in range(8):
        u0, u1 = gap[:, cp * 256:cp * 256 + 128], gap[:, cp * 256 + 128:cp * 256 + 256]
        dist_ref[2 * cp:2 * cp + 1, :] = jnp.where(half_row, u0, pltpu.roll(u1, 64, 1))
        dist_ref[2 * cp + 1:2 * cp + 2, :] = jnp.where(half_row, pltpu.roll(u0, 64, 1), u1)

    for k in (1, 3, 2):
        recv("xa%d" % k, xr.at[k - 1])
    xf[y] = xf[y] + xr[0].astype(F32) + xr[1].astype(F32) + xr[2].astype(F32)
    for k in (2, 1, 3):
        zs[k - 1] = xf[y, lax.rem(zh + k, 4)].astype(BF16)
        send("xz%d" % k, zs.at[k - 1], zr.at[k - 1], to_zh(k))
    out = xf[y, zh]
    for k in (1, 3, 2):
        recv("xz%d" % k, zr.at[k - 1])
        out = out + zr[k - 1].astype(F32)
    cross_ref[...] = out.T

    for copy in outs:
        copy.wait()
    for copy in pending:
        copy.wait_send()


def per_device(vectors, rotation, codebook, codes):
    vmem = pl.BlockSpec(memory_space=pltpu.VMEM)
    hbm = pl.BlockSpec(memory_space=pltpu.HBM)
    cent, dist, cross = pl.pallas_call(
        kernel,
        out_shape=(
            jax.ShapeDtypeStruct((K, DS), BF16),
            jax.ShapeDtypeStruct((16, 128), F32),
            jax.ShapeDtypeStruct((DS, DS), F32),
        ),
        in_specs=[hbm] * 4,
        out_specs=(pl.BlockSpec(memory_space=pl.ANY), vmem, vmem),
        scratch_shapes=[
            pltpu.VMEM((GROUP, D), BF16),
            pltpu.VMEM((4, GROUP, DS), BF16),
            pltpu.VMEM((GROUP, DS), BF16),
            pltpu.VMEM((DS, GROUP), F32),
            pltpu.VMEM((D, DS), BF16),
            pltpu.VMEM((D, DS), BF16),
            pltpu.VMEM((16, 128), jnp.int32),
            pltpu.VMEM((4, 16, 128), jnp.int32),
            pltpu.VMEM((256, 4 * GROUP), BF16),
            pltpu.VMEM((4, GROUP, DS), BF16),
            pltpu.VMEM((5, 16, 256), F32),
            pltpu.VMEM((256, 4 * DS), F32),
            pltpu.VMEM((3, OWN, DS), BF16),
            pltpu.VMEM((3, OWN, DS), BF16),
            pltpu.VMEM((OWN, DS), F32),
            pltpu.VMEM((OWN, DS), BF16),
            pltpu.VMEM((K, DS), BF16),
            pltpu.VMEM((DS, GROUP), F32),
            pltpu.VMEM((DS, GROUP), BF16),
            pltpu.VMEM((4, 4, DS, 128), F32),
            pltpu.VMEM((3, 4, DS, 128), BF16),
            pltpu.VMEM((3, 4, DS, 128), BF16),
            pltpu.VMEM((3, DS, 128), BF16),
            pltpu.VMEM((3, DS, 128), BF16),
            pltpu.SemaphoreType.DMA((SEMS,)),
            pltpu.SemaphoreType.DMA((SEMS,)),
            pltpu.SemaphoreType.DMA((21,)),
        ],
        compiler_params=pltpu.CompilerParams(
            collective_id=0, has_side_effects=True, vmem_limit_bytes=48 * 1024 * 1024
        ),
        name="opq_step",
    )(vectors, rotation, codebook.reshape(K, DS), codes.reshape(16, 128))
    return cent.reshape(1, K, DS), dist.reshape(GROUP, 1), cross


def solution(mesh):
    placed = (P(("dp", "sub"), None), P(None, "sub"), P("sub", None, None), P("dp", "sub"))
    return jax.shard_map(
        per_device,
        mesh=mesh,
        in_specs=placed,
        out_specs=(P("sub", None, None), P("dp", "sub"), P("dp", "sub")),
        check_vma=False,
    )
```

```python
import jax
import jax.numpy as jnp
from jax import lax
from jax.experimental import pallas as pl
from jax.experimental.pallas import tpu as pltpu
from jax.sharding import PartitionSpec as P

BF16 = jnp.bfloat16
F32 = jnp.float32
MESH = pl.DeviceIdType.MESH

D = 2048
K = 4096
DS = 128
GROUP = 2048
OWN = 256
SEMS = 160


def kernel(
    v_ref, r_ref, cb_ref, codes_ref,
    cent_out, dist_ref, cross_ref,
    vg, rot, oth, rott, rown, roth, raw, codes, lo, hicol, counts, tacc, tsend, trecv, cnt, cbk, cent,
    reb, rebb, xf, xs, xr, zs, zr,
    ssem, rsem, lsem,
):
    dp = lax.axis_index("dp")
    sub = lax.axis_index("sub")
    zh, y = lax.div(dp, 4), lax.rem(dp, 4)
    x, zl, core = lax.div(sub, 4), lax.rem(lax.div(sub, 2), 2), lax.rem(sub, 2)
    xp, xm, x2 = lax.rem(x + 1, 4), lax.rem(x + 3, 4), lax.rem(x + 2, 4)
    yp, ym, y2 = lax.rem(y + 1, 4), lax.rem(y + 3, 4), lax.rem(y + 2, 4)
    zo, co = 1 - zl, 1 - core

    def sid(a, b, c):
        return a * 4 + b * 2 + c

    to_xp, to_xm = (dp, sid(xp, zl, core)), (dp, sid(xm, zl, core))
    to_z = (dp, sid(x, zo, core))
    to_core = (dp, sid(x, zl, co))
    to_out = (lax.rem(zh + 3 + 2 * zl, 4) * 4 + y, sid(x, zo, core))

    def to_y(k):
        return (zh * 4 + lax.rem(y + k, 4), sub)

    def to_zh(k):
        return (lax.rem(zh + k, 4) * 4 + y, sub)

    pending = []
    ids = {}

    def role(name):
        return ids.setdefault(name, len(ids))

    def send(name, src, dst, target):
        i = role(name)
        copy = pltpu.make_async_remote_copy(
            src_ref=src, dst_ref=dst, send_sem=ssem.at[i], recv_sem=rsem.at[i],
            device_id=target, device_id_type=MESH,
        )
        copy.start()
        pending.append(copy)

    def recv(name, ref):
        i = role(name)
        pltpu.make_async_remote_copy(
            src_ref=ref, dst_ref=ref, send_sem=ssem.at[i], recv_sem=rsem.at[i],
            device_id=to_core, device_id_type=MESH,
        ).wait_recv()

    def piece(cp, h, c):
        return pl.ds(pl.multiple_of(cp * 256 + h * 128 + c * 64, 64), 64)

    def unit(cp, h):
        return pl.ds(pl.multiple_of(cp * 256 + h * 128, 128), 128)

    def chip(cp):
        return pl.ds(pl.multiple_of(cp * 256, 256), 256)

    here, up, down, far = x * 2 + zl, xp * 2 + zl, xm * 2 + zl, x2 * 2 + zl
    here_z, up_z, down_z, far_z = x * 2 + zo, xp * 2 + zo, xm * 2 + zo, x2 * 2 + zo

    local = [
        pltpu.make_async_copy(v_ref.at[pl.ds(h * 64, 64)], vg.at[piece(here, h, core)], lsem.at[h])
        for h in range(2)
    ]
    local.append(pltpu.make_async_copy(codes_ref, raw, lsem.at[2]))
    local.append(pltpu.make_async_copy(r_ref, rown, lsem.at[3]))
    hi_own = 4 * y + zh
    own_rows = pl.ds(pl.multiple_of(hi_own * OWN, OWN), OWN)
    local.append(pltpu.make_async_copy(cb_ref.at[own_rows], cbk, lsem.at[4]))
    for copy in local:
        copy.start()

    barrier = pltpu.get_barrier_semaphore()
    peers = [to_xp, to_xm, to_z, to_core, to_out] + [to_y(k) for k in (1, 3, 2)] + [to_zh(k) for k in (1, 3, 2)]
    for peer in peers:
        pl.semaphore_signal(barrier, inc=1, device_id=peer, device_id_type=MESH)
    for copy in local:
        copy.wait()

    even, odd = raw[pl.ds(0, 8, stride=2), :], raw[pl.ds(1, 8, stride=2), :]
    first = lax.broadcasted_iota(jnp.int32, (8, 128), 1) < 64
    codes[y, 0:8, :] = jnp.where(first, even, pltpu.roll(odd, 64, 1))
    codes[y, 8:16, :] = jnp.where(first, pltpu.roll(even, 64, 1), odd)
    pl.semaphore_wait(barrier, len(peers))

    def vsend(name, cp, h, c, target):
        ref = vg.at[piece(cp, h, c)]
        send(name, ref, ref, target)

    def vrecv(name, cp, h, c):
        recv(name, vg.at[piece(cp, h, c)])

    vsend("xm0", here, 0, core, to_xp)
    vsend("xp1", here, 1, core, to_xm)
    top, low = pl.ds(0, 1024), pl.ds(1024, 1024)
    send("r_in", rown.at[top], roth.at[top], to_z)
    send("r_out", rown.at[low], roth.at[low], to_out)
    for h in range(2):
        vsend("d_own%d" % h, here, h, core, to_core)
    for k in (1, 3, 2):
        send("code%d" % k, codes.at[y], codes.at[y], to_y(k))
    vsend("xm1", here, 1, core, to_xp)
    vsend("xp0", here, 0, core, to_xm)

    def y_send(name, rows, direct):
        ref = rot.at[y, rows]
        send("a" + name, ref, ref, to_y(1))
        send("b" + name, ref, ref, to_y(3))
        if direct:
            send("c" + name, ref, ref, to_y(2))

    def halves(start, size):
        a = pl.ds(pl.multiple_of(start, 64), size)
        b = pl.ds(pl.multiple_of(start + size, 64), size)
        return a, b

    def y_forward(name, start, size):
        rows = pl.ds(pl.multiple_of(start, 128), size)
        a, b = halves(start, size // 2)
        recv("a" + name, rot.at[ym, rows])
        ref = rot.at[ym, a]
        send("c" + name, ref, ref, to_y(1))
        recv("b" + name, rot.at[yp, rows])
        ref = rot.at[yp, b]
        send("d" + name, ref, ref, to_y(3))

    def y_last(name, start, size, direct):
        if direct:
            rows = pl.ds(pl.multiple_of(start, 128), size)
            recv("a" + name, rot.at[ym, rows])
            recv("b" + name, rot.at[yp, rows])
            recv("c" + name, rot.at[y2, rows])
        else:
            a, b = halves(start, size // 2)
            recv("c" + name, rot.at[y2, a])
            recv("d" + name, rot.at[y2, b])

    def rot_own(rows):
        part = jnp.dot(vg[rows, :], rown[...], preferred_element_type=F32)
        rot[y, rows, :] = part.astype(BF16)

    def rot_oth(rows):
        part = jnp.dot(vg[rows, :], roth[...], preferred_element_type=F32)
        oth[rows, :] = part.astype(BF16)

    def rot_both(rows):
        both = jnp.concatenate([rown[...], roth[...]], axis=1)
        part = jnp.dot(vg[rows, :], both, preferred_element_type=F32)
        rot[y, rows, :] = part[:, :DS].astype(BF16)
        oth[rows, :] = part[:, DS:].astype(BF16)

    def z_send(name, rows):
        send("z" + name, oth.at[rows], rot.at[y, rows], to_z)

    def z_recv(name, rows):
        recv("z" + name, rot.at[y, rows])

    for h in range(2):
        vrecv("d_own%d" % h, here, h, co)
    rot_own(chip(here))
    y_send("A", chip(here), False)

    for k in (1, 3, 2):
        recv("code%d" % k, codes.at[lax.rem(y + 4 - k, 4)])
    tacc[...] = jnp.zeros_like(tacc)
    iota = lax.broadcasted_iota(jnp.int32, (256, 128), 0)

    def lo_table(g, carry):
        tile = jnp.bitwise_and(codes[g], 255)
        for i in range(16):
            cp, h = i // 2, i % 2
            row = tile[h * 8 + cp:h * 8 + cp + 1, :]
            mark = jnp.where(iota == jnp.broadcast_to(row, (256, 128)), 1.0, 0.0)
            lo[:, pl.ds(pl.multiple_of(g * GROUP + i * 128, 128), 128)] = mark.astype(BF16)
        return carry

    lax.fori_loop(0, 4, lo_table, 0)

    def hi_table(g, carry):
        tile = lax.shift_right_logical(codes[g], 8).astype(F32)
        for i in range(16):
            cp, h = i // 2, i % 2
            row = tile[h * 8 + cp:h * 8 + cp + 1, :]
            hicol[g, i * 128:(i + 1) * 128, :] = jnp.broadcast_to(row, (128, 128)).T.astype(BF16)
        return carry

    vrecv("xm0", down, 0, core)
    vsend("x20", down, 0, core, to_xp)
    vsend("d_xm0", down, 0, core, to_core)
    vrecv("xp1", up, 1, core)
    vsend("x21", up, 1, core, to_xm)
    vsend("d_xp1", up, 1, core, to_core)
    recv("r_in", roth.at[top])
    recv("r_out", roth.at[low])
    rot_oth(chip(here))
    z_send("A", chip(here))
    vrecv("d_xm0", down, 0, co)
    rot_both(unit(down, 0))
    y_send("B", unit(down, 0), False)
    z_send("B", unit(down, 0))
    vrecv("d_xp1", up, 1, co)
    rot_both(unit(up, 1))
    y_send("C", unit(up, 1), False)
    z_send("C", unit(up, 1))
    vsend("w0", here, 0, core, to_z)
    y_forward("A", here * 256, 256)
    lax.fori_loop(0, 4, hi_table, 0)

    z_recv("A", chip(here_z))
    y_send("Az", chip(here_z), False)
    z_recv("B", unit(down_z, 0))
    y_send("Bz", unit(down_z, 0), False)
    z_recv("C", unit(up_z, 1))
    y_send("Cz", unit(up_z, 1), False)
    y_forward("B", down * 256, 128)
    y_forward("C", up * 256 + 128, 128)

    def count(g, acc):
        for h in range(2):
            for cp in range(8):
                row = lax.shift_right_logical(codes[g, h * 8 + cp:h * 8 + cp + 1, :], 8)
                mark = jnp.where(iota[:16] == jnp.broadcast_to(row, (16, 128)), 1.0, 0.0).astype(BF16)
                tab = lo[:, pl.ds(pl.multiple_of(g * GROUP + (cp * 2 + h) * 128, 128), 128)]
                acc = acc + lax.dot_general(mark, tab, (((1,), (1,)), ((), ())), preferred_element_type=F32)
        return acc

    counts[0] = lax.fori_loop(0, 4, count, jnp.zeros((16, 256), F32))
    for k in (1, 3, 2):
        send("n%d" % k, counts.at[0], counts.at[k], to_zh(k))

    vrecv("xm1", down, 1, core)
    vsend("d_xm1", down, 1, core, to_core)
    vrecv("xp0", up, 0, core)
    vsend("d_xp0", up, 0, core, to_core)
    vrecv("d_xm1", down, 1, co)
    rot_both(unit(down, 1))
    y_send("D", unit(down, 1), False)
    z_send("D", unit(down, 1))
    vrecv("d_xp0", up, 0, co)
    rot_both(unit(up, 0))
    y_send("E", unit(up, 0), False)
    z_send("E", unit(up, 0))
    vsend("w1", here, 1, core, to_z)
    y_forward("Az", here_z * 256, 256)
    y_forward("Bz", down_z * 256, 128)
    y_forward("Cz", up_z * 256 + 128, 128)

    def accumulate(cp):
        marks, wides = [], []
        for g in range(4):
            marks.append(lo[:, pl.ds(pl.multiple_of(g * GROUP + cp * 256, 256), 256)])
            values = rot[g, chip(cp), :]
            his = hicol[g, chip(cp), :]
            parts = []
            for h in range(4):
                want = (4 * y + h).astype(F32).astype(BF16)
                parts.append(jnp.where(his == want, values, jnp.zeros_like(values)))
            wides.append(jnp.concatenate(parts, axis=1))
        mark, wide = jnp.concatenate(marks, axis=1), jnp.concatenate(wides, axis=0)
        tacc[...] += jnp.dot(mark, wide, preferred_element_type=F32)

    y_last("A", here * 256, 256, False)
    accumulate(here)
    z_recv("D", unit(down_z, 1))
    y_send("Dz", unit(down_z, 1), False)
    z_recv("E", unit(up_z, 0))
    y_send("Ez", unit(up_z, 0), False)
    y_forward("D", down * 256 + 128, 128)
    y_forward("E", up * 256, 128)
    y_last("Az", here_z * 256, 256, False)
    accumulate(here_z)

    vrecv("x20", far, 0, core)
    vsend("d_x20", far, 0, core, to_core)
    vrecv("x21", far, 1, core)
    vsend("d_x21", far, 1, core, to_core)
    for h in range(2):
        vrecv("d_x2%d" % h, far, h, co)
    rot_both(chip(far))
    z_send("F", chip(far))
    y_send("F", chip(far), True)
    y_forward("Dz", down_z * 256 + 128, 128)
    y_forward("Ez", up_z * 256, 128)

    vrecv("w0", here_z, 0, core)
    vsend("wm0", here_z, 0, core, to_xp)
    vsend("wp0", here_z, 0, core, to_xm)
    vsend("d_w0", here_z, 0, core, to_core)
    z_recv("F", chip(far_z))
    y_send("Fz", chip(far_z), True)
    y_last("B", down * 256, 128, False)
    y_last("D", down * 256 + 128, 128, False)
    accumulate(down)
    y_last("C", up * 256 + 128, 128, False)
    y_last("E", up * 256, 128, False)
    accumulate(up)
    vrecv("w1", here_z, 1, core)
    vsend("wp1", here_z, 1, core, to_xm)
    vsend("wm1", here_z, 1, core, to_xp)
    vsend("d_w1", here_z, 1, core, to_core)
    y_last("Bz", down_z * 256, 128, False)
    y_last("Dz", down_z * 256 + 128, 128, False)
    accumulate(down_z)
    y_last("Cz", up_z * 256 + 128, 128, False)
    y_last("Ez", up_z * 256, 128, False)
    accumulate(up_z)
    y_last("F", far * 256, 256, True)
    accumulate(far)
    y_last("Fz", far_z * 256, 256, True)
    accumulate(far_z)

    for k in (2, 1, 3):
        theirs = pl.ds(pl.multiple_of(lax.rem(zh + k, 4) * DS, DS), DS)
        tsend[k - 1] = tacc[:, theirs].astype(BF16)
        send("t%d" % k, tsend.at[k - 1], trecv.at[k - 1], to_zh(k))
    for k in (1, 3, 2):
        recv("n%d" % k, counts.at[k])
    number = counts[0] + counts[1] + counts[2] + counts[3]
    counts[4] = number
    mine = counts[4, pl.ds(hi_own, 1), :]
    cnt[...] = jnp.broadcast_to(mine, (128, 256)).T
    rott[...] = rot[y].astype(F32).T
    vrecv("wm0", down_z, 0, core)
    vsend("w20", down_z, 0, core, to_xp)
    vsend("d_wm0", down_z, 0, core, to_core)
    vrecv("wp1", up_z, 1, core)
    vsend("w21", up_z, 1, core, to_xm)
    vsend("d_wp1", up_z, 1, core, to_core)
    total = tacc[:, pl.ds(pl.multiple_of(zh * DS, DS), DS)]
    for k in (1, 3, 2):
        recv("t%d" % k, trecv.at[k - 1])
        total = total + trecv[k - 1].astype(F32)
    cent[own_rows, :] = ((total + cbk[...].astype(F32)) / (cnt[...] + 1.0)).astype(BF16)

    def chunk(a, b):
        return pl.ds(pl.multiple_of(b * 1024 + a * OWN, OWN), OWN)

    def half_chunk(a, b, h):
        return pl.ds(pl.multiple_of(b * 1024 + a * OWN + h * 128, 128), 128)

    outs = []

    def rebuild(a, b):
        copy = pltpu.make_async_copy(
            cent.at[chunk(a, b)], cent_out.at[chunk(a, b)], lsem.at[5 + len(outs)]
        )
        copy.start()
        outs.append(copy)
        table = cent[chunk(a, b), :].astype(F32).T.astype(BF16)
        want = 4 * b + a
        for i in range(8):
            tab = lo[:, pl.ds(pl.multiple_of(y * GROUP + i * 256, 256), 256)]
            got = jnp.dot(table, tab, preferred_element_type=F32)
            place = slice(i * 256, (i + 1) * 256)
            row = jnp.concatenate([codes[y, i:i + 1, :], codes[y, i + 8:i + 9, :]], axis=1)
            hit = lax.shift_right_logical(row, 8) == want
            reb[:, place] = jnp.where(jnp.broadcast_to(hit, (128, 256)), got, reb[:, place])

    def y_chunk_send(q, a):
        ref = cent.at[chunk(a, y)]
        send("ca%d" % q, ref, ref, to_y(1))
        send("cb%d" % q, ref, ref, to_y(3))

    def y_chunk_forward(q, a):
        recv("ca%d" % q, cent.at[chunk(a, ym)])
        ref = cent.at[half_chunk(a, ym, 0)]
        send("cc%d" % q, ref, ref, to_y(1))
        recv("cb%d" % q, cent.at[chunk(a, yp)])
        ref = cent.at[half_chunk(a, yp, 1)]
        send("cd%d" % q, ref, ref, to_y(3))

    reb[...] = jnp.zeros_like(reb)
    zs_of = [zh] + [lax.rem(zh + 4 - q, 4) for q in (1, 2, 3)]
    for k in (2, 1, 3):
        ref = cent.at[own_rows]
        send("cz%d" % k, ref, ref, to_zh(k))
    y_chunk_send(0, zh)
    rebuild(zh, y)
    y_chunk_forward(0, zh)
    order = (1, 3, 2)
    before = 0
    for q in order:
        a = zs_of[q]
        recv("cz%d" % q, cent.at[chunk(a, y)])
        y_chunk_send(q, a)
        if before:
            y_chunk_forward(before, zs_of[before])
        rebuild(a, y)
        rebuild(zs_of[before], ym)
        rebuild(zs_of[before], yp)
        before = q
    y_chunk_forward(before, zs_of[before])
    for b in (ym, yp):
        rebuild(zs_of[before], b)

    vrecv("wm1", down_z, 1, core)
    vsend("d_wm1", down_z, 1, core, to_core)
    vrecv("wp0", up_z, 0, core)
    vsend("d_wp0", up_z, 0, core, to_core)
    vrecv("w20", far_z, 0, core)
    vsend("d_w20", far_z, 0, core, to_core)
    vrecv("w21", far_z, 1, core)
    vsend("d_w21", far_z, 1, core, to_core)
    for q in (0,) + order:
        a = zs_of[q]
        recv("cc%d" % q, cent.at[half_chunk(a, y2, 0)])
        recv("cd%d" % q, cent.at[half_chunk(a, y2, 1)])
        rebuild(a, y2)
    for h in range(2):
        vrecv("d_w%d" % h, here_z, h, co)
        vrecv("d_wm%d" % h, down_z, h, co)
        vrecv("d_wp%d" % h, up_z, h, co)
        vrecv("d_w2%d" % h, far_z, h, co)

    rebb[...] = reb[...].astype(BF16)

    def cross_half(p):
        def body(i, carry):
            place = pl.ds(pl.multiple_of(i * 512 + p * 256, 256), 256)
            part = jnp.dot(rebb[...], vg[:, place], preferred_element_type=F32)
            xf[2 * p, i] = part[:, :128]
            xf[2 * p + 1, i] = part[:, 128:]
            return carry

        lax.fori_loop(0, 4, body, 0)

    def cross_send(k):
        xs[k - 1] = xf[lax.rem(y + k, 4)].astype(BF16)
        send("xa%d" % k, xs.at[k - 1], xr.at[k - 1], to_y(k))

    near = lax.div(y, 2)
    cross_half(1 - near)
    cross_send(2)
    cross_half(near)
    cross_send(1)
    cross_send(3)

    gap = rott[...] - reb[...]
    gap = jnp.sum(gap * gap, axis=0, keepdims=True)
    half_row = lax.broadcasted_iota(jnp.int32, (1, 128), 1) < 64
    for cp in range(8):
        u0, u1 = gap[:, cp * 256:cp * 256 + 128], gap[:, cp * 256 + 128:cp * 256 + 256]
        dist_ref[2 * cp:2 * cp + 1, :] = jnp.where(half_row, u0, pltpu.roll(u1, 64, 1))
        dist_ref[2 * cp + 1:2 * cp + 2, :] = jnp.where(half_row, pltpu.roll(u0, 64, 1), u1)

    for k in (1, 3, 2):
        recv("xa%d" % k, xr.at[k - 1])
    xf[y] = xf[y] + xr[0].astype(F32) + xr[1].astype(F32) + xr[2].astype(F32)
    for k in (2, 1, 3):
        zs[k - 1] = xf[y, lax.rem(zh + k, 4)].astype(BF16)
        send("xz%d" % k, zs.at[k - 1], zr.at[k - 1], to_zh(k))
    out = xf[y, zh]
    for k in (1, 3, 2):
        recv("xz%d" % k, zr.at[k - 1])
        out = out + zr[k - 1].astype(F32)
    cross_ref[...] = out.T

    for copy in outs:
        copy.wait()
    for copy in pending:
        copy.wait_send()


def per_device(vectors, rotation, codebook, codes):
    vmem = pl.BlockSpec(memory_space=pltpu.VMEM)
    hbm = pl.BlockSpec(memory_space=pltpu.HBM)
    operands = (vectors, rotation, codebook.reshape(K, DS), codes.reshape(16, 128))
    cent, dist, cross = pl.pallas_call(
        kernel,
        out_shape=(
            jax.ShapeDtypeStruct((K, DS), BF16),
            jax.ShapeDtypeStruct((16, 128), F32),
            jax.ShapeDtypeStruct((DS, DS), F32),
        ),
        in_specs=[hbm] * 4,
        out_specs=(pl.BlockSpec(memory_space=pl.ANY), vmem, vmem),
        scratch_shapes=[
            pltpu.VMEM((GROUP, D), BF16),
            pltpu.VMEM((4, GROUP, DS), BF16),
            pltpu.VMEM((GROUP, DS), BF16),
            pltpu.VMEM((DS, GROUP), F32),
            pltpu.VMEM((D, DS), BF16),
            pltpu.VMEM((D, DS), BF16),
            pltpu.VMEM((16, 128), jnp.int32),
            pltpu.VMEM((4, 16, 128), jnp.int32),
            pltpu.VMEM((256, 4 * GROUP), BF16),
            pltpu.VMEM((4, GROUP, DS), BF16),
            pltpu.VMEM((5, 16, 256), F32),
            pltpu.VMEM((256, 4 * DS), F32),
            pltpu.VMEM((3, OWN, DS), BF16),
            pltpu.VMEM((3, OWN, DS), BF16),
            pltpu.VMEM((OWN, DS), F32),
            pltpu.VMEM((OWN, DS), BF16),
            pltpu.VMEM((K, DS), BF16),
            pltpu.VMEM((DS, GROUP), F32),
            pltpu.VMEM((DS, GROUP), BF16),
            pltpu.VMEM((4, 4, DS, 128), F32),
            pltpu.VMEM((3, 4, DS, 128), BF16),
            pltpu.VMEM((3, 4, DS, 128), BF16),
            pltpu.VMEM((3, DS, 128), BF16),
            pltpu.VMEM((3, DS, 128), BF16),
            pltpu.SemaphoreType.DMA((SEMS,)),
            pltpu.SemaphoreType.DMA((SEMS,)),
            pltpu.SemaphoreType.DMA((21,)),
        ],
        compiler_params=pltpu.CompilerParams(
            collective_id=0, has_side_effects=True, vmem_limit_bytes=48 * 1024 * 1024
        ),
        name="opq_step",
    )(*(pltpu.with_memory_space_constraint(t, pltpu.HBM) for t in operands))
    return cent.reshape(1, K, DS), dist.reshape(GROUP, 1), cross


def solution(mesh):
    placed = (P(("dp", "sub"), None), P(None, "sub"), P("sub", None, None), P("dp", "sub"))
    return jax.shard_map(
        per_device,
        mesh=mesh,
        in_specs=placed,
        out_specs=(P("sub", None, None), P("dp", "sub"), P("dp", "sub")),
        check_vma=False,
    )
```

```python
import jax
import jax.numpy as jnp
from jax import lax
from jax.experimental import pallas as pl
from jax.experimental.pallas import tpu as pltpu
from jax.sharding import PartitionSpec as P

BF16 = jnp.bfloat16
F32 = jnp.float32
MESH = pl.DeviceIdType.MESH

D = 2048
K = 4096
DS = 128
GROUP = 2048
OWN = 256
SEMS = 192


def kernel(
    v_ref, r_ref, cb_ref, codes_ref,
    cent_out, dist_ref, cross_ref,
    vg, rot, oth, rott, rown, roth, raw, codes, lo, hicol, counts, tacc, tsend, trecv, cnt, cbk, cent,
    reb, rebb, xf, xs, xr, zs, zr,
    ssem, rsem, lsem,
):
    dp = lax.axis_index("dp")
    sub = lax.axis_index("sub")
    zh, y = lax.div(dp, 4), lax.rem(dp, 4)
    x, zl, core = lax.div(sub, 4), lax.rem(lax.div(sub, 2), 2), lax.rem(sub, 2)
    xp, xm, x2 = lax.rem(x + 1, 4), lax.rem(x + 3, 4), lax.rem(x + 2, 4)
    yp, ym, y2 = lax.rem(y + 1, 4), lax.rem(y + 3, 4), lax.rem(y + 2, 4)
    zo, co = 1 - zl, 1 - core

    def sid(a, b, c):
        return a * 4 + b * 2 + c

    to_xp, to_xm = (dp, sid(xp, zl, core)), (dp, sid(xm, zl, core))
    to_z = (dp, sid(x, zo, core))
    to_core = (dp, sid(x, zl, co))
    to_out = (lax.rem(zh + 3 + 2 * zl, 4) * 4 + y, sid(x, zo, core))

    def to_y(k):
        return (zh * 4 + lax.rem(y + k, 4), sub)

    def to_zh(k):
        return (lax.rem(zh + k, 4) * 4 + y, sub)

    pending = []
    ids = {}

    def role(name):
        return ids.setdefault(name, len(ids))

    def send(name, src, dst, target):
        i = role(name)
        copy = pltpu.make_async_remote_copy(
            src_ref=src, dst_ref=dst, send_sem=ssem.at[i], recv_sem=rsem.at[i],
            device_id=target, device_id_type=MESH,
        )
        copy.start()
        pending.append(copy)

    def recv(name, ref):
        i = role(name)
        pltpu.make_async_remote_copy(
            src_ref=ref, dst_ref=ref, send_sem=ssem.at[i], recv_sem=rsem.at[i],
            device_id=to_core, device_id_type=MESH,
        ).wait_recv()

    def piece(cp, h, c):
        return pl.ds(pl.multiple_of(cp * 256 + h * 128 + c * 64, 64), 64)

    def unit(cp, h):
        return pl.ds(pl.multiple_of(cp * 256 + h * 128, 128), 128)

    def chip(cp):
        return pl.ds(pl.multiple_of(cp * 256, 256), 256)

    here, up, down, far = x * 2 + zl, xp * 2 + zl, xm * 2 + zl, x2 * 2 + zl
    here_z, up_z, down_z, far_z = x * 2 + zo, xp * 2 + zo, xm * 2 + zo, x2 * 2 + zo

    local = [
        pltpu.make_async_copy(v_ref.at[pl.ds(h * 64, 64)], vg.at[piece(here, h, core)], lsem.at[h])
        for h in range(2)
    ]
    local.append(pltpu.make_async_copy(codes_ref, raw, lsem.at[2]))
    local.append(pltpu.make_async_copy(r_ref, rown, lsem.at[3]))
    hi_own = 4 * y + zh
    own_rows = pl.ds(pl.multiple_of(hi_own * OWN, OWN), OWN)
    local.append(pltpu.make_async_copy(cb_ref.at[own_rows], cbk, lsem.at[4]))
    for copy in local:
        copy.start()

    barrier = pltpu.get_barrier_semaphore()
    peers = [to_xp, to_xm, to_z, to_core, to_out] + [to_y(k) for k in (1, 3, 2)] + [to_zh(k) for k in (1, 3, 2)]
    for peer in peers:
        pl.semaphore_signal(barrier, inc=1, device_id=peer, device_id_type=MESH)
    for copy in local:
        copy.wait()

    even, odd = raw[pl.ds(0, 8, stride=2), :], raw[pl.ds(1, 8, stride=2), :]
    first = lax.broadcasted_iota(jnp.int32, (8, 128), 1) < 64
    codes[y, 0:8, :] = jnp.where(first, even, pltpu.roll(odd, 64, 1))
    codes[y, 8:16, :] = jnp.where(first, pltpu.roll(even, 64, 1), odd)
    pl.semaphore_wait(barrier, len(peers))

    def vsend(name, cp, h, c, target):
        ref = vg.at[piece(cp, h, c)]
        send(name, ref, ref, target)

    def vrecv(name, cp, h, c):
        recv(name, vg.at[piece(cp, h, c)])

    vsend("xm0", here, 0, core, to_xp)
    vsend("xp0", here, 0, core, to_xm)
    top, low = pl.ds(0, 1024), pl.ds(1024, 1024)
    send("r_in", rown.at[top], roth.at[top], to_z)
    send("r_out", rown.at[low], roth.at[low], to_out)
    for h in range(2):
        vsend("d_own%d" % h, here, h, core, to_core)
    for k in (1, 3, 2):
        send("code%d" % k, codes.at[y], codes.at[y], to_y(k))
    vsend("xm1", here, 1, core, to_xp)
    vsend("xp1", here, 1, core, to_xm)

    def quarter(cp, h, v, c):
        return vg.at[pl.ds(pl.multiple_of(cp * 256 + h * 128 + c * 64 + v * 32, 32), 32)]

    def x_forward(h):
        vrecv("xm%d" % h, down, h, core)
        ref = quarter(down, h, 0, core)
        send("xf%d" % h, ref, ref, to_xp)
        vsend("d_xm%d" % h, down, h, core, to_core)
        vrecv("xp%d" % h, up, h, core)
        ref = quarter(up, h, 1, core)
        send("xg%d" % h, ref, ref, to_xm)
        vsend("d_xp%d" % h, up, h, core, to_core)

    def x_far(h):
        recv("xf%d" % h, quarter(far, h, 0, core))
        recv("xg%d" % h, quarter(far, h, 1, core))
        vsend("d_x2%d" % h, far, h, core, to_core)
        vrecv("d_x2%d" % h, far, h, co)

    def y_send(name, rows, direct):
        ref = rot.at[y, rows]
        send("a" + name, ref, ref, to_y(1))
        send("b" + name, ref, ref, to_y(3))
        if direct:
            send("c" + name, ref, ref, to_y(2))

    def halves(start, size):
        a = pl.ds(pl.multiple_of(start, 64), size)
        b = pl.ds(pl.multiple_of(start + size, 64), size)
        return a, b

    def y_forward(name, start, size):
        rows = pl.ds(pl.multiple_of(start, 128), size)
        a, b = halves(start, size // 2)
        recv("a" + name, rot.at[ym, rows])
        ref = rot.at[ym, a]
        send("c" + name, ref, ref, to_y(1))
        recv("b" + name, rot.at[yp, rows])
        ref = rot.at[yp, b]
        send("d" + name, ref, ref, to_y(3))

    def y_last(name, start, size, direct):
        if direct:
            rows = pl.ds(pl.multiple_of(start, 128), size)
            recv("a" + name, rot.at[ym, rows])
            recv("b" + name, rot.at[yp, rows])
            recv("c" + name, rot.at[y2, rows])
        else:
            a, b = halves(start, size // 2)
            recv("c" + name, rot.at[y2, a])
            recv("d" + name, rot.at[y2, b])

    def rot_own(rows):
        part = jnp.dot(vg[rows, :], rown[...], preferred_element_type=F32)
        rot[y, rows, :] = part.astype(BF16)

    def rot_oth(rows):
        part = jnp.dot(vg[rows, :], roth[...], preferred_element_type=F32)
        oth[rows, :] = part.astype(BF16)

    def rot_both(rows):
        both = jnp.concatenate([rown[...], roth[...]], axis=1)
        part = jnp.dot(vg[rows, :], both, preferred_element_type=F32)
        rot[y, rows, :] = part[:, :DS].astype(BF16)
        oth[rows, :] = part[:, DS:].astype(BF16)

    def z_send(name, rows):
        send("z" + name, oth.at[rows], rot.at[y, rows], to_z)

    def z_recv(name, rows):
        recv("z" + name, rot.at[y, rows])

    for h in range(2):
        vrecv("d_own%d" % h, here, h, co)
    rot_own(chip(here))
    y_send("A", chip(here), False)

    for k in (1, 3, 2):
        recv("code%d" % k, codes.at[lax.rem(y + 4 - k, 4)])
    tacc[...] = jnp.zeros_like(tacc)
    iota = lax.broadcasted_iota(jnp.int32, (256, 128), 0)

    def lo_table(g, carry):
        tile = jnp.bitwise_and(codes[g], 255)
        for i in range(16):
            cp, h = i // 2, i % 2
            row = tile[h * 8 + cp:h * 8 + cp + 1, :]
            mark = jnp.where(iota == jnp.broadcast_to(row, (256, 128)), 1.0, 0.0)
            lo[:, pl.ds(pl.multiple_of(g * GROUP + i * 128, 128), 128)] = mark.astype(BF16)
        return carry

    lax.fori_loop(0, 4, lo_table, 0)

    def hi_table(g, carry):
        tile = lax.shift_right_logical(codes[g], 8).astype(F32)
        for i in range(16):
            cp, h = i // 2, i % 2
            row = tile[h * 8 + cp:h * 8 + cp + 1, :]
            hicol[g, i * 128:(i + 1) * 128, :] = jnp.broadcast_to(row, (128, 128)).T.astype(BF16)
        return carry

    x_forward(0)
    recv("r_in", roth.at[top])
    recv("r_out", roth.at[low])
    rot_oth(chip(here))
    z_send("A", chip(here))
    vrecv("d_xm0", down, 0, co)
    rot_both(unit(down, 0))
    y_send("B", unit(down, 0), False)
    z_send("B", unit(down, 0))
    vrecv("d_xp0", up, 0, co)
    rot_both(unit(up, 0))
    y_send("C", unit(up, 0), False)
    z_send("C", unit(up, 0))
    y_forward("A", here * 256, 256)
    lax.fori_loop(0, 4, hi_table, 0)

    z_recv("A", chip(here_z))
    y_send("Az", chip(here_z), False)
    z_recv("B", unit(down_z, 0))
    y_send("Bz", unit(down_z, 0), False)
    z_recv("C", unit(up_z, 0))
    y_send("Cz", unit(up_z, 0), False)
    y_forward("B", down * 256, 128)
    y_forward("C", up * 256, 128)

    def count(g, acc):
        for h in range(2):
            for cp in range(8):
                row = lax.shift_right_logical(codes[g, h * 8 + cp:h * 8 + cp + 1, :], 8)
                mark = jnp.where(iota[:16] == jnp.broadcast_to(row, (16, 128)), 1.0, 0.0).astype(BF16)
                tab = lo[:, pl.ds(pl.multiple_of(g * GROUP + (cp * 2 + h) * 128, 128), 128)]
                acc = acc + lax.dot_general(mark, tab, (((1,), (1,)), ((), ())), preferred_element_type=F32)
        return acc

    counts[0] = lax.fori_loop(0, 4, count, jnp.zeros((16, 256), F32))
    for k in (1, 3, 2):
        send("n%d" % k, counts.at[0], counts.at[k], to_zh(k))

    x_forward(1)
    vrecv("d_xm1", down, 1, co)
    rot_both(unit(down, 1))
    y_send("D", unit(down, 1), False)
    z_send("D", unit(down, 1))
    vrecv("d_xp1", up, 1, co)
    rot_both(unit(up, 1))
    y_send("E", unit(up, 1), False)
    z_send("E", unit(up, 1))
    y_forward("Az", here_z * 256, 256)
    y_forward("Bz", down_z * 256, 128)
    y_forward("Cz", up_z * 256, 128)

    def accumulate(cp):
        marks, wides = [], []
        for g in range(4):
            marks.append(lo[:, pl.ds(pl.multiple_of(g * GROUP + cp * 256, 256), 256)])
            values = rot[g, chip(cp), :]
            his = hicol[g, chip(cp), :]
            parts = []
            for h in range(4):
                want = (4 * y + h).astype(F32).astype(BF16)
                parts.append(jnp.where(his == want, values, jnp.zeros_like(values)))
            wides.append(jnp.concatenate(parts, axis=1))
        mark, wide = jnp.concatenate(marks, axis=1), jnp.concatenate(wides, axis=0)
        tacc[...] += jnp.dot(mark, wide, preferred_element_type=F32)

    y_last("A", here * 256, 256, False)
    accumulate(here)
    x_far(0)
    rot_both(unit(far, 0))
    z_send("F", unit(far, 0))
    y_send("F", unit(far, 0), True)
    z_recv("D", unit(down_z, 1))
    y_send("Dz", unit(down_z, 1), False)
    z_recv("E", unit(up_z, 1))
    y_send("Ez", unit(up_z, 1), False)
    y_forward("D", down * 256 + 128, 128)
    y_forward("E", up * 256 + 128, 128)

    x_far(1)
    rot_both(unit(far, 1))
    z_send("G", unit(far, 1))
    y_send("G", unit(far, 1), True)
    vsend("w0", here, 0, core, to_z)
    vsend("w1", here, 1, core, to_z)
    z_recv("F", unit(far_z, 0))
    y_send("Fz", unit(far_z, 0), True)
    y_forward("Dz", down_z * 256 + 128, 128)
    y_forward("Ez", up_z * 256 + 128, 128)
    z_recv("G", unit(far_z, 1))
    y_send("Gz", unit(far_z, 1), True)
    y_last("Az", here_z * 256, 256, False)
    accumulate(here_z)
    y_last("B", down * 256, 128, False)
    y_last("D", down * 256 + 128, 128, False)
    accumulate(down)
    y_last("C", up * 256, 128, False)
    y_last("E", up * 256 + 128, 128, False)
    accumulate(up)
    y_last("Bz", down_z * 256, 128, False)
    y_last("Dz", down_z * 256 + 128, 128, False)
    accumulate(down_z)
    y_last("Cz", up_z * 256, 128, False)
    y_last("Ez", up_z * 256 + 128, 128, False)
    accumulate(up_z)
    vrecv("w0", here_z, 0, core)
    vsend("wm0", here_z, 0, core, to_xp)
    vsend("wp0", here_z, 0, core, to_xm)
    vsend("d_w0", here_z, 0, core, to_core)
    y_last("F", far * 256, 128, True)
    y_last("G", far * 256 + 128, 128, True)
    accumulate(far)
    y_last("Fz", far_z * 256, 128, True)
    y_last("Gz", far_z * 256 + 128, 128, True)
    accumulate(far_z)

    def part(hb):
        return pl.ds(hb * 128, 128)

    for hb in range(2):
        for k in (2, 1, 3):
            theirs = pl.ds(pl.multiple_of(lax.rem(zh + k, 4) * DS, DS), DS)
            tsend[k - 1, part(hb), :] = tacc[part(hb), theirs].astype(BF16)
            send("t%d%d" % (k, hb), tsend.at[k - 1, part(hb)], trecv.at[k - 1, part(hb)], to_zh(k))
    for k in (1, 3, 2):
        recv("n%d" % k, counts.at[k])
    counts[4] = counts[0] + counts[1] + counts[2] + counts[3]
    mine = counts[4, pl.ds(hi_own, 1), :]
    cnt[...] = jnp.broadcast_to(mine, (128, 256)).T
    rott[...] = rot[y].astype(F32).T
    vrecv("w1", here_z, 1, core)
    vsend("wp1", here_z, 1, core, to_xm)
    vsend("wm1", here_z, 1, core, to_xp)
    vsend("d_w1", here_z, 1, core, to_core)

    def chunk(a, b):
        return pl.ds(pl.multiple_of(b * 1024 + a * OWN, OWN), OWN)

    def half_chunk(a, b, hb):
        return pl.ds(pl.multiple_of(b * 1024 + a * OWN + hb * 128, 128), 128)

    def quarter_chunk(a, b, hb, v):
        return pl.ds(pl.multiple_of(b * 1024 + a * OWN + hb * 128 + v * 64, 64), 64)

    def y_chunk_send(q, hb):
        ref = cent.at[half_chunk(zs_of[q], y, hb)]
        send("ca%d%d" % (q, hb), ref, ref, to_y(1))
        send("cb%d%d" % (q, hb), ref, ref, to_y(3))

    def y_chunk_forward(q, hb):
        a = zs_of[q]
        recv("ca%d%d" % (q, hb), cent.at[half_chunk(a, ym, hb)])
        ref = cent.at[quarter_chunk(a, ym, hb, 0)]
        send("cc%d%d" % (q, hb), ref, ref, to_y(1))
        recv("cb%d%d" % (q, hb), cent.at[half_chunk(a, yp, hb)])
        ref = cent.at[quarter_chunk(a, yp, hb, 1)]
        send("cd%d%d" % (q, hb), ref, ref, to_y(3))

    def z_chunk(q, hb):
        recv("cz%d%d" % (q, hb), cent.at[half_chunk(zs_of[q], y, hb)])
        y_chunk_send(q, hb)

    zs_of = [zh] + [lax.rem(zh + 4 - q, 4) for q in (1, 2, 3)]
    for hb in range(2):
        total = tacc[part(hb), pl.ds(pl.multiple_of(zh * DS, DS), DS)]
        for k in (1, 3, 2):
            recv("t%d%d" % (k, hb), trecv.at[k - 1, part(hb)])
            total = total + trecv[k - 1, part(hb), :].astype(F32)
        value = (total + cbk[part(hb), :].astype(F32)) / (cnt[part(hb), :] + 1.0)
        cent[half_chunk(zh, y, hb), :] = value.astype(BF16)
        ref = cent.at[half_chunk(zh, y, hb)]
        for k in (1, 3, 2):
            send("cz%d%d" % (k, hb), ref, ref, to_zh(k))
        y_chunk_send(0, hb)

    outs = []

    def rebuild(a, b):
        copy = pltpu.make_async_copy(
            cent.at[chunk(a, b)], cent_out.at[chunk(a, b)], lsem.at[5 + len(outs)]
        )
        copy.start()
        outs.append(copy)
        table = cent[chunk(a, b), :].astype(F32).T.astype(BF16)
        want = 4 * b + a
        for i in range(8):
            tab = lo[:, pl.ds(pl.multiple_of(y * GROUP + i * 256, 256), 256)]
            got = jnp.dot(table, tab, preferred_element_type=F32)
            place = slice(i * 256, (i + 1) * 256)
            row = jnp.concatenate([codes[y, i:i + 1, :], codes[y, i + 8:i + 9, :]], axis=1)
            hit = lax.shift_right_logical(row, 8) == want
            reb[:, place] = jnp.where(jnp.broadcast_to(hit, (128, 256)), got, reb[:, place])

    reb[...] = jnp.zeros_like(reb)
    vrecv("wm0", down_z, 0, core)
    vsend("w20", down_z, 0, core, to_xp)
    vsend("d_wm0", down_z, 0, core, to_core)
    vrecv("wp0", up_z, 0, core)
    vsend("d_wp0", up_z, 0, core, to_core)
    y_chunk_forward(0, 0)
    z_chunk(1, 0)
    z_chunk(3, 0)
    y_chunk_forward(0, 1)
    rebuild(zh, y)
    z_chunk(2, 0)
    y_chunk_forward(1, 0)
    y_chunk_forward(3, 0)
    rebuild(zh, ym)
    rebuild(zh, yp)
    vrecv("wp1", up_z, 1, core)
    vsend("w21", up_z, 1, core, to_xm)
    vsend("d_wp1", up_z, 1, core, to_core)
    vrecv("wm1", down_z, 1, core)
    vsend("d_wm1", down_z, 1, core, to_core)
    z_chunk(1, 1)
    z_chunk(3, 1)
    y_chunk_forward(2, 0)
    z_chunk(2, 1)
    rebuild(zs_of[1], y)
    rebuild(zs_of[3], y)
    y_chunk_forward(1, 1)
    y_chunk_forward(3, 1)
    rebuild(zs_of[2], y)
    y_chunk_forward(2, 1)
    for q in (1, 3, 2):
        rebuild(zs_of[q], ym)
        rebuild(zs_of[q], yp)

    vrecv("w20", far_z, 0, core)
    vsend("d_w20", far_z, 0, core, to_core)
    vrecv("w21", far_z, 1, core)
    vsend("d_w21", far_z, 1, core, to_core)
    for q in (0, 1, 3, 2):
        a = zs_of[q]
        for hb in range(2):
            recv("cc%d%d" % (q, hb), cent.at[quarter_chunk(a, y2, hb, 0)])
            recv("cd%d%d" % (q, hb), cent.at[quarter_chunk(a, y2, hb, 1)])
        rebuild(a, y2)
    for h in range(2):
        vrecv("d_w%d" % h, here_z, h, co)
        vrecv("d_wm%d" % h, down_z, h, co)
        vrecv("d_wp%d" % h, up_z, h, co)
        vrecv("d_w2%d" % h, far_z, h, co)

    rebb[...] = reb[...].astype(BF16)

    pairs = ((2, 1), (3, 0))

    def cross_part(k, p):
        to = lax.rem(y + k, 4)
        blocks = []
        for z in pairs[p]:
            column = (lax.rem(zh + z, 4) * 4 + to) * 128
            blocks.append(vg[:, pl.ds(pl.multiple_of(column, 128), 128)])
        got = jnp.dot(rebb[...], jnp.concatenate(blocks, axis=1), preferred_element_type=F32)
        if k == 0:
            xf[p, 0] = got[:, :128]
            xf[p, 1] = got[:, 128:]
        else:
            xs[k - 1, p, 0] = got[:, :128].astype(BF16)
            xs[k - 1, p, 1] = got[:, 128:].astype(BF16)
            send("xa%d%d" % (k, p), xs.at[k - 1, p], xr.at[k - 1, p], to_y(k))

    for p in range(2):
        for k in (2, 1, 3):
            cross_part(k, p)
    for p in range(2):
        cross_part(0, p)

    gap = rott[...] - reb[...]
    gap = jnp.sum(gap * gap, axis=0, keepdims=True)
    half_row = lax.broadcasted_iota(jnp.int32, (1, 128), 1) < 64
    for cp in range(8):
        u0, u1 = gap[:, cp * 256:cp * 256 + 128], gap[:, cp * 256 + 128:cp * 256 + 256]
        dist_ref[2 * cp:2 * cp + 1, :] = jnp.where(half_row, u0, pltpu.roll(u1, 64, 1))
        dist_ref[2 * cp + 1:2 * cp + 2, :] = jnp.where(half_row, pltpu.roll(u0, 64, 1), u1)

    def cross_sum(p):
        for k in (1, 3, 2):
            recv("xa%d%d" % (k, p), xr.at[k - 1, p])
        return [xf[p, i] + xr[0, p, i].astype(F32) + xr[1, p, i].astype(F32) + xr[2, p, i].astype(F32) for i in range(2)]

    def cross_zh(k, value):
        zs[k - 1] = value.astype(BF16)
        send("xz%d" % k, zs.at[k - 1], zr.at[k - 1], to_zh(k))

    two, one = cross_sum(0)
    cross_zh(2, two)
    cross_zh(1, one)
    three, out = cross_sum(1)
    cross_zh(3, three)
    for k in (1, 2, 3):
        recv("xz%d" % k, zr.at[k - 1])
        out = out + zr[k - 1].astype(F32)
    cross_ref[...] = out.T

    for copy in outs:
        copy.wait()
    for copy in pending:
        copy.wait_send()


def per_device(vectors, rotation, codebook, codes):
    vmem = pl.BlockSpec(memory_space=pltpu.VMEM)
    hbm = pl.BlockSpec(memory_space=pltpu.HBM)
    operands = (vectors, rotation, codebook.reshape(K, DS), codes.reshape(16, 128))
    cent, dist, cross = pl.pallas_call(
        kernel,
        out_shape=(
            jax.ShapeDtypeStruct((K, DS), BF16),
            jax.ShapeDtypeStruct((16, 128), F32),
            jax.ShapeDtypeStruct((DS, DS), F32),
        ),
        in_specs=[hbm] * 4,
        out_specs=(pl.BlockSpec(memory_space=pl.ANY), vmem, vmem),
        scratch_shapes=[
            pltpu.VMEM((GROUP, D), BF16),
            pltpu.VMEM((4, GROUP, DS), BF16),
            pltpu.VMEM((GROUP, DS), BF16),
            pltpu.VMEM((DS, GROUP), F32),
            pltpu.VMEM((D, DS), BF16),
            pltpu.VMEM((D, DS), BF16),
            pltpu.VMEM((16, 128), jnp.int32),
            pltpu.VMEM((4, 16, 128), jnp.int32),
            pltpu.VMEM((256, 4 * GROUP), BF16),
            pltpu.VMEM((4, GROUP, DS), BF16),
            pltpu.VMEM((5, 16, 256), F32),
            pltpu.VMEM((256, 4 * DS), F32),
            pltpu.VMEM((3, OWN, DS), BF16),
            pltpu.VMEM((3, OWN, DS), BF16),
            pltpu.VMEM((OWN, DS), F32),
            pltpu.VMEM((OWN, DS), BF16),
            pltpu.VMEM((K, DS), BF16),
            pltpu.VMEM((DS, GROUP), F32),
            pltpu.VMEM((DS, GROUP), BF16),
            pltpu.VMEM((2, 2, DS, 128), F32),
            pltpu.VMEM((3, 2, 2, DS, 128), BF16),
            pltpu.VMEM((3, 2, 2, DS, 128), BF16),
            pltpu.VMEM((3, DS, 128), BF16),
            pltpu.VMEM((3, DS, 128), BF16),
            pltpu.SemaphoreType.DMA((SEMS,)),
            pltpu.SemaphoreType.DMA((SEMS,)),
            pltpu.SemaphoreType.DMA((21,)),
        ],
        compiler_params=pltpu.CompilerParams(
            collective_id=0, has_side_effects=True, vmem_limit_bytes=48 * 1024 * 1024
        ),
        name="opq_step",
    )(*(pltpu.with_memory_space_constraint(t, pltpu.HBM) for t in operands))
    return cent.reshape(1, K, DS), dist.reshape(GROUP, 1), cross


def solution(mesh):
    placed = (P(("dp", "sub"), None), P(None, "sub"), P("sub", None, None), P("dp", "sub"))
    return jax.shard_map(
        per_device,
        mesh=mesh,
        in_specs=placed,
        out_specs=(P("sub", None, None), P("dp", "sub"), P("dp", "sub")),
        check_vma=False,
    )
```

```python
import jax
import jax.numpy as jnp
from jax import lax
from jax.experimental import pallas as pl
from jax.experimental.pallas import tpu as pltpu
from jax.sharding import PartitionSpec as P

BF16 = jnp.bfloat16
F32 = jnp.float32
MESH = pl.DeviceIdType.MESH

D = 2048
K = 4096
DS = 128
GROUP = 2048
OWN = 256
SEMS = 192


def kernel(
    v_ref, r_ref, cb_ref, codes_ref,
    cent_out, dist_ref, cross_ref,
    vg, rot, oth, rott, rown, roth, raw, codes, lo, hicol, counts, tacc, tsend, trecv, cnt, cbk, cent,
    reb, rebb, xf, xs, xr, zs, zr,
    ssem, rsem, lsem,
):
    dp = lax.axis_index("dp")
    sub = lax.axis_index("sub")
    zh, y = lax.div(dp, 4), lax.rem(dp, 4)
    x, zl, core = lax.div(sub, 4), lax.rem(lax.div(sub, 2), 2), lax.rem(sub, 2)
    xp, xm, x2 = lax.rem(x + 1, 4), lax.rem(x + 3, 4), lax.rem(x + 2, 4)
    yp, ym, y2 = lax.rem(y + 1, 4), lax.rem(y + 3, 4), lax.rem(y + 2, 4)
    zo, co = 1 - zl, 1 - core

    def sid(a, b, c):
        return a * 4 + b * 2 + c

    to_xp, to_xm = (dp, sid(xp, zl, core)), (dp, sid(xm, zl, core))
    to_z = (dp, sid(x, zo, core))
    to_core = (dp, sid(x, zl, co))
    to_out = (lax.rem(zh + 3 + 2 * zl, 4) * 4 + y, sid(x, zo, core))

    def to_y(k):
        return (zh * 4 + lax.rem(y + k, 4), sub)

    def to_zh(k):
        return (lax.rem(zh + k, 4) * 4 + y, sub)

    pending = []
    ids = {}

    def role(name):
        return ids.setdefault(name, len(ids))

    def send(name, src, dst, target):
        i = role(name)
        copy = pltpu.make_async_remote_copy(
            src_ref=src, dst_ref=dst, send_sem=ssem.at[i], recv_sem=rsem.at[i],
            device_id=target, device_id_type=MESH,
        )
        copy.start()
        pending.append(copy)

    def recv(name, ref):
        i = role(name)
        pltpu.make_async_remote_copy(
            src_ref=ref, dst_ref=ref, send_sem=ssem.at[i], recv_sem=rsem.at[i],
            device_id=to_core, device_id_type=MESH,
        ).wait_recv()

    def piece(cp, h, c):
        return pl.ds(pl.multiple_of(cp * 256 + h * 128 + c * 64, 64), 64)

    def unit(cp, h):
        return pl.ds(pl.multiple_of(cp * 256 + h * 128, 128), 128)

    def chip(cp):
        return pl.ds(pl.multiple_of(cp * 256, 256), 256)

    here, up, down, far = x * 2 + zl, xp * 2 + zl, xm * 2 + zl, x2 * 2 + zl
    here_z, up_z, down_z, far_z = x * 2 + zo, xp * 2 + zo, xm * 2 + zo, x2 * 2 + zo

    local = [
        pltpu.make_async_copy(v_ref.at[pl.ds(h * 64, 64)], vg.at[piece(here, h, core)], lsem.at[h])
        for h in range(2)
    ]
    local.append(pltpu.make_async_copy(codes_ref, raw, lsem.at[2]))
    local.append(pltpu.make_async_copy(r_ref, rown, lsem.at[3]))
    hi_own = 4 * y + zh
    own_rows = pl.ds(pl.multiple_of(hi_own * OWN, OWN), OWN)
    local.append(pltpu.make_async_copy(cb_ref.at[own_rows], cbk, lsem.at[4]))
    for copy in local:
        copy.start()

    barrier = pltpu.get_barrier_semaphore()
    peers = [to_xp, to_xm, to_z, to_core, to_out] + [to_y(k) for k in (1, 3, 2)] + [to_zh(k) for k in (1, 3, 2)]
    for peer in peers:
        pl.semaphore_signal(barrier, inc=1, device_id=peer, device_id_type=MESH)
    for copy in local:
        copy.wait()

    even, odd = raw[pl.ds(0, 8, stride=2), :], raw[pl.ds(1, 8, stride=2), :]
    first = lax.broadcasted_iota(jnp.int32, (8, 128), 1) < 64
    codes[y, 0:8, :] = jnp.where(first, even, pltpu.roll(odd, 64, 1))
    codes[y, 8:16, :] = jnp.where(first, pltpu.roll(even, 64, 1), odd)
    pl.semaphore_wait(barrier, len(peers))

    def vsend(name, cp, h, c, target):
        ref = vg.at[piece(cp, h, c)]
        send(name, ref, ref, target)

    def vrecv(name, cp, h, c):
        recv(name, vg.at[piece(cp, h, c)])

    vsend("xm0", here, 0, core, to_xp)
    vsend("xp0", here, 0, core, to_xm)
    top, low = pl.ds(0, 1024), pl.ds(1024, 1024)
    send("r_in", rown.at[top], roth.at[top], to_z)
    send("r_out", rown.at[low], roth.at[low], to_out)
    for h in range(2):
        vsend("d_own%d" % h, here, h, core, to_core)
    for k in (1, 3, 2):
        send("code%d" % k, codes.at[y], codes.at[y], to_y(k))
    vsend("xm1", here, 1, core, to_xp)
    vsend("xp1", here, 1, core, to_xm)

    def quarter(cp, h, v, c):
        return vg.at[pl.ds(pl.multiple_of(cp * 256 + h * 128 + c * 64 + v * 32, 32), 32)]

    def x_forward(h):
        vrecv("xm%d" % h, down, h, core)
        ref = quarter(down, h, 0, core)
        send("xf%d" % h, ref, ref, to_xp)
        vsend("d_xm%d" % h, down, h, core, to_core)
        vrecv("xp%d" % h, up, h, core)
        ref = quarter(up, h, 1, core)
        send("xg%d" % h, ref, ref, to_xm)
        vsend("d_xp%d" % h, up, h, core, to_core)

    def x_far(h):
        recv("xf%d" % h, quarter(far, h, 0, core))
        recv("xg%d" % h, quarter(far, h, 1, core))
        vsend("d_x2%d" % h, far, h, core, to_core)
        vrecv("d_x2%d" % h, far, h, co)

    def y_send(name, rows, direct):
        ref = rot.at[y, rows]
        send("a" + name, ref, ref, to_y(1))
        send("b" + name, ref, ref, to_y(3))
        if direct:
            send("c" + name, ref, ref, to_y(2))

    def halves(start, size):
        a = pl.ds(pl.multiple_of(start, 64), size)
        b = pl.ds(pl.multiple_of(start + size, 64), size)
        return a, b

    def y_forward(name, start, size):
        rows = pl.ds(pl.multiple_of(start, 128), size)
        a, b = halves(start, size // 2)
        recv("a" + name, rot.at[ym, rows])
        ref = rot.at[ym, a]
        send("c" + name, ref, ref, to_y(1))
        recv("b" + name, rot.at[yp, rows])
        ref = rot.at[yp, b]
        send("d" + name, ref, ref, to_y(3))

    def y_last(name, start, size, direct):
        if direct:
            rows = pl.ds(pl.multiple_of(start, 128), size)
            recv("a" + name, rot.at[ym, rows])
            recv("b" + name, rot.at[yp, rows])
            recv("c" + name, rot.at[y2, rows])
        else:
            a, b = halves(start, size // 2)
            recv("c" + name, rot.at[y2, a])
            recv("d" + name, rot.at[y2, b])

    def rot_own(rows):
        part = jnp.dot(vg[rows, :], rown[...], preferred_element_type=F32)
        rot[y, rows, :] = part.astype(BF16)

    def rot_oth(rows):
        part = jnp.dot(vg[rows, :], roth[...], preferred_element_type=F32)
        oth[rows, :] = part.astype(BF16)

    def rot_both(rows):
        both = jnp.concatenate([rown[...], roth[...]], axis=1)
        part = jnp.dot(vg[rows, :], both, preferred_element_type=F32)
        rot[y, rows, :] = part[:, :DS].astype(BF16)
        oth[rows, :] = part[:, DS:].astype(BF16)

    def z_send(name, rows):
        send("z" + name, oth.at[rows], rot.at[y, rows], to_z)

    def z_recv(name, rows):
        recv("z" + name, rot.at[y, rows])

    for h in range(2):
        vrecv("d_own%d" % h, here, h, co)
    rot_own(chip(here))
    y_send("A", chip(here), False)

    for k in (1, 3, 2):
        recv("code%d" % k, codes.at[lax.rem(y + 4 - k, 4)])
    tacc[...] = jnp.zeros_like(tacc)
    iota = lax.broadcasted_iota(jnp.int32, (256, 128), 0)

    def lo_table(g, carry):
        tile = jnp.bitwise_and(codes[g], 255)
        for i in range(16):
            cp, h = i // 2, i % 2
            row = tile[h * 8 + cp:h * 8 + cp + 1, :]
            mark = jnp.where(iota == jnp.broadcast_to(row, (256, 128)), 1.0, 0.0)
            lo[:, pl.ds(pl.multiple_of(g * GROUP + i * 128, 128), 128)] = mark.astype(BF16)
        return carry

    lax.fori_loop(0, 4, lo_table, 0)

    def hi_table(g, carry):
        tile = lax.shift_right_logical(codes[g], 8).astype(F32)
        for i in range(16):
            cp, h = i // 2, i % 2
            row = tile[h * 8 + cp:h * 8 + cp + 1, :]
            hicol[g, i * 128:(i + 1) * 128, :] = jnp.broadcast_to(row, (128, 128)).T.astype(BF16)
        return carry

    x_forward(0)
    recv("r_in", roth.at[top])
    recv("r_out", roth.at[low])
    rot_oth(chip(here))
    z_send("A", chip(here))
    vrecv("d_xm0", down, 0, co)
    rot_both(unit(down, 0))
    y_send("B", unit(down, 0), False)
    z_send("B", unit(down, 0))
    vrecv("d_xp0", up, 0, co)
    rot_both(unit(up, 0))
    y_send("C", unit(up, 0), False)
    z_send("C", unit(up, 0))
    vsend("w0", here, 0, core, to_z)
    y_forward("A", here * 256, 256)
    lax.fori_loop(0, 4, hi_table, 0)

    z_recv("A", chip(here_z))
    y_send("Az", chip(here_z), False)
    z_recv("B", unit(down_z, 0))
    y_send("Bz", unit(down_z, 0), False)
    z_recv("C", unit(up_z, 0))
    y_send("Cz", unit(up_z, 0), False)
    y_forward("B", down * 256, 128)
    y_forward("C", up * 256, 128)

    def count(g, acc):
        for h in range(2):
            for cp in range(8):
                row = lax.shift_right_logical(codes[g, h * 8 + cp:h * 8 + cp + 1, :], 8)
                mark = jnp.where(iota[:16] == jnp.broadcast_to(row, (16, 128)), 1.0, 0.0).astype(BF16)
                tab = lo[:, pl.ds(pl.multiple_of(g * GROUP + (cp * 2 + h) * 128, 128), 128)]
                acc = acc + lax.dot_general(mark, tab, (((1,), (1,)), ((), ())), preferred_element_type=F32)
        return acc

    counts[0] = lax.fori_loop(0, 4, count, jnp.zeros((16, 256), F32))
    for k in (1, 3, 2):
        send("n%d" % k, counts.at[0], counts.at[k], to_zh(k))

    x_forward(1)
    vrecv("d_xm1", down, 1, co)
    rot_both(unit(down, 1))
    y_send("D", unit(down, 1), False)
    z_send("D", unit(down, 1))
    vrecv("d_xp1", up, 1, co)
    rot_both(unit(up, 1))
    y_send("E", unit(up, 1), False)
    z_send("E", unit(up, 1))
    y_forward("Az", here_z * 256, 256)
    y_forward("Bz", down_z * 256, 128)
    y_forward("Cz", up_z * 256, 128)

    def accumulate(cp):
        marks, wides = [], []
        for g in range(4):
            marks.append(lo[:, pl.ds(pl.multiple_of(g * GROUP + cp * 256, 256), 256)])
            values = rot[g, chip(cp), :]
            his = hicol[g, chip(cp), :]
            parts = []
            for h in range(4):
                want = (4 * y + h).astype(F32).astype(BF16)
                parts.append(jnp.where(his == want, values, jnp.zeros_like(values)))
            wides.append(jnp.concatenate(parts, axis=1))
        mark, wide = jnp.concatenate(marks, axis=1), jnp.concatenate(wides, axis=0)
        tacc[...] += jnp.dot(mark, wide, preferred_element_type=F32)

    y_last("A", here * 256, 256, False)
    accumulate(here)
    x_far(0)
    rot_both(unit(far, 0))
    z_send("F", unit(far, 0))
    y_send("F", unit(far, 0), True)
    z_recv("D", unit(down_z, 1))
    y_send("Dz", unit(down_z, 1), False)
    z_recv("E", unit(up_z, 1))
    y_send("Ez", unit(up_z, 1), False)
    y_forward("D", down * 256 + 128, 128)
    y_forward("E", up * 256 + 128, 128)

    x_far(1)
    rot_both(unit(far, 1))
    z_send("G", unit(far, 1))
    y_send("G", unit(far, 1), True)
    vsend("w1", here, 1, core, to_z)
    vrecv("w0", here_z, 0, core)
    vsend("wm0", here_z, 0, core, to_xp)
    vsend("wp0", here_z, 0, core, to_xm)
    vsend("d_w0", here_z, 0, core, to_core)
    z_recv("F", unit(far_z, 0))
    y_send("Fz", unit(far_z, 0), True)
    y_forward("Dz", down_z * 256 + 128, 128)
    y_forward("Ez", up_z * 256 + 128, 128)
    z_recv("G", unit(far_z, 1))
    y_send("Gz", unit(far_z, 1), True)
    y_last("Az", here_z * 256, 256, False)
    accumulate(here_z)
    y_last("B", down * 256, 128, False)
    y_last("D", down * 256 + 128, 128, False)
    accumulate(down)
    y_last("C", up * 256, 128, False)
    y_last("E", up * 256 + 128, 128, False)
    accumulate(up)
    y_last("Bz", down_z * 256, 128, False)
    y_last("Dz", down_z * 256 + 128, 128, False)
    accumulate(down_z)
    y_last("Cz", up_z * 256, 128, False)
    y_last("Ez", up_z * 256 + 128, 128, False)
    accumulate(up_z)
    vrecv("w1", here_z, 1, core)
    vsend("wp1", here_z, 1, core, to_xm)
    vsend("wm1", here_z, 1, core, to_xp)
    vsend("d_w1", here_z, 1, core, to_core)
    vrecv("wm0", down_z, 0, core)
    vsend("w20", down_z, 0, core, to_xp)
    vsend("d_wm0", down_z, 0, core, to_core)
    vrecv("wp0", up_z, 0, core)
    vsend("d_wp0", up_z, 0, core, to_core)
    y_last("F", far * 256, 128, True)
    y_last("G", far * 256 + 128, 128, True)
    accumulate(far)
    y_last("Fz", far_z * 256, 128, True)
    y_last("Gz", far_z * 256 + 128, 128, True)
    accumulate(far_z)

    def part(hb):
        return pl.ds(hb * 128, 128)

    for hb in range(2):
        for k in (2, 1, 3):
            theirs = pl.ds(pl.multiple_of(lax.rem(zh + k, 4) * DS, DS), DS)
            tsend[k - 1, part(hb), :] = tacc[part(hb), theirs].astype(BF16)
            send("t%d%d" % (k, hb), tsend.at[k - 1, part(hb)], trecv.at[k - 1, part(hb)], to_zh(k))
    for k in (1, 3, 2):
        recv("n%d" % k, counts.at[k])
    counts[4] = counts[0] + counts[1] + counts[2] + counts[3]
    mine = counts[4, pl.ds(hi_own, 1), :]
    cnt[...] = jnp.broadcast_to(mine, (128, 256)).T
    rott[...] = rot[y].astype(F32).T
    vrecv("wp1", up_z, 1, core)
    vsend("w21", up_z, 1, core, to_xm)
    vsend("d_wp1", up_z, 1, core, to_core)
    vrecv("wm1", down_z, 1, core)
    vsend("d_wm1", down_z, 1, core, to_core)

    def chunk(a, b):
        return pl.ds(pl.multiple_of(b * 1024 + a * OWN, OWN), OWN)

    def half_chunk(a, b, hb):
        return pl.ds(pl.multiple_of(b * 1024 + a * OWN + hb * 128, 128), 128)

    def quarter_chunk(a, b, hb, v):
        return pl.ds(pl.multiple_of(b * 1024 + a * OWN + hb * 128 + v * 64, 64), 64)

    def y_chunk_send(q, hb):
        ref = cent.at[half_chunk(zs_of[q], y, hb)]
        send("ca%d%d" % (q, hb), ref, ref, to_y(1))
        send("cb%d%d" % (q, hb), ref, ref, to_y(3))

    def y_chunk_forward(q, hb):
        a = zs_of[q]
        recv("ca%d%d" % (q, hb), cent.at[half_chunk(a, ym, hb)])
        ref = cent.at[quarter_chunk(a, ym, hb, 0)]
        send("cc%d%d" % (q, hb), ref, ref, to_y(1))
        recv("cb%d%d" % (q, hb), cent.at[half_chunk(a, yp, hb)])
        ref = cent.at[quarter_chunk(a, yp, hb, 1)]
        send("cd%d%d" % (q, hb), ref, ref, to_y(3))

    def z_chunk(q, hb):
        recv("cz%d%d" % (q, hb), cent.at[half_chunk(zs_of[q], y, hb)])
        y_chunk_send(q, hb)

    zs_of = [zh] + [lax.rem(zh + 4 - q, 4) for q in (1, 2, 3)]
    for hb in range(2):
        total = tacc[part(hb), pl.ds(pl.multiple_of(zh * DS, DS), DS)]
        for k in (1, 3, 2):
            recv("t%d%d" % (k, hb), trecv.at[k - 1, part(hb)])
            total = total + trecv[k - 1, part(hb), :].astype(F32)
        value = (total + cbk[part(hb), :].astype(F32)) / (cnt[part(hb), :] + 1.0)
        cent[half_chunk(zh, y, hb), :] = value.astype(BF16)
        ref = cent.at[half_chunk(zh, y, hb)]
        for k in (1, 3, 2):
            send("cz%d%d" % (k, hb), ref, ref, to_zh(k))
        y_chunk_send(0, hb)

    outs = []

    def rebuild(a, b):
        copy = pltpu.make_async_copy(
            cent.at[chunk(a, b)], cent_out.at[chunk(a, b)], lsem.at[5 + len(outs)]
        )
        copy.start()
        outs.append(copy)
        table = cent[chunk(a, b), :].astype(F32).T.astype(BF16)
        want = 4 * b + a
        for i in range(8):
            tab = lo[:, pl.ds(pl.multiple_of(y * GROUP + i * 256, 256), 256)]
            got = jnp.dot(table, tab, preferred_element_type=F32)
            place = slice(i * 256, (i + 1) * 256)
            row = jnp.concatenate([codes[y, i:i + 1, :], codes[y, i + 8:i + 9, :]], axis=1)
            hit = lax.shift_right_logical(row, 8) == want
            reb[:, place] = jnp.where(jnp.broadcast_to(hit, (128, 256)), got, reb[:, place])

    reb[...] = jnp.zeros_like(reb)
    y_chunk_forward(0, 0)
    z_chunk(1, 0)
    z_chunk(3, 0)
    y_chunk_forward(0, 1)
    rebuild(zh, y)
    z_chunk(2, 0)
    y_chunk_forward(1, 0)
    y_chunk_forward(3, 0)
    rebuild(zh, ym)
    rebuild(zh, yp)
    z_chunk(1, 1)
    z_chunk(3, 1)
    y_chunk_forward(2, 0)
    z_chunk(2, 1)
    rebuild(zs_of[1], y)
    rebuild(zs_of[3], y)
    y_chunk_forward(1, 1)
    y_chunk_forward(3, 1)
    rebuild(zs_of[2], y)
    y_chunk_forward(2, 1)
    for q in (1, 3, 2):
        rebuild(zs_of[q], ym)
        rebuild(zs_of[q], yp)

    vrecv("w20", far_z, 0, core)
    vsend("d_w20", far_z, 0, core, to_core)
    vrecv("w21", far_z, 1, core)
    vsend("d_w21", far_z, 1, core, to_core)
    for q in (0, 1, 3, 2):
        a = zs_of[q]
        for hb in range(2):
            recv("cc%d%d" % (q, hb), cent.at[quarter_chunk(a, y2, hb, 0)])
            recv("cd%d%d" % (q, hb), cent.at[quarter_chunk(a, y2, hb, 1)])
        rebuild(a, y2)
    for h in range(2):
        vrecv("d_w%d" % h, here_z, h, co)
        vrecv("d_wm%d" % h, down_z, h, co)
        vrecv("d_wp%d" % h, up_z, h, co)
        vrecv("d_w2%d" % h, far_z, h, co)

    rebb[...] = reb[...].astype(BF16)

    pairs = ((2, 1), (3, 0))

    def cross_part(k, p):
        to = lax.rem(y + k, 4)
        blocks = []
        for z in pairs[p]:
            column = (lax.rem(zh + z, 4) * 4 + to) * 128
            blocks.append(vg[:, pl.ds(pl.multiple_of(column, 128), 128)])
        got = jnp.dot(rebb[...], jnp.concatenate(blocks, axis=1), preferred_element_type=F32)
        if k == 0:
            xf[p, 0] = got[:, :128]
            xf[p, 1] = got[:, 128:]
        else:
            xs[k - 1, p, 0] = got[:, :128].astype(BF16)
            xs[k - 1, p, 1] = got[:, 128:].astype(BF16)
            send("xa%d%d" % (k, p), xs.at[k - 1, p], xr.at[k - 1, p], to_y(k))

    for p in range(2):
        for k in (2, 1, 3):
            cross_part(k, p)
    for p in range(2):
        cross_part(0, p)

    gap = rott[...] - reb[...]
    gap = jnp.sum(gap * gap, axis=0, keepdims=True)
    half_row = lax.broadcasted_iota(jnp.int32, (1, 128), 1) < 64
    for cp in range(8):
        u0, u1 = gap[:, cp * 256:cp * 256 + 128], gap[:, cp * 256 + 128:cp * 256 + 256]
        dist_ref[2 * cp:2 * cp + 1, :] = jnp.where(half_row, u0, pltpu.roll(u1, 64, 1))
        dist_ref[2 * cp + 1:2 * cp + 2, :] = jnp.where(half_row, pltpu.roll(u0, 64, 1), u1)

    def cross_sum(p):
        for k in (1, 3, 2):
            recv("xa%d%d" % (k, p), xr.at[k - 1, p])
        return [xf[p, i] + xr[0, p, i].astype(F32) + xr[1, p, i].astype(F32) + xr[2, p, i].astype(F32) for i in range(2)]

    def cross_zh(k, value):
        zs[k - 1] = value.astype(BF16)
        send("xz%d" % k, zs.at[k - 1], zr.at[k - 1], to_zh(k))

    two, one = cross_sum(0)
    cross_zh(2, two)
    cross_zh(1, one)
    three, out = cross_sum(1)
    cross_zh(3, three)
    for k in (1, 2, 3):
        recv("xz%d" % k, zr.at[k - 1])
        out = out + zr[k - 1].astype(F32)
    cross_ref[...] = out.T

    for copy in outs:
        copy.wait()
    for copy in pending:
        copy.wait_send()


def per_device(vectors, rotation, codebook, codes):
    vmem = pl.BlockSpec(memory_space=pltpu.VMEM)
    hbm = pl.BlockSpec(memory_space=pltpu.HBM)
    operands = (vectors, rotation, codebook.reshape(K, DS), codes.reshape(16, 128))
    cent, dist, cross = pl.pallas_call(
        kernel,
        out_shape=(
            jax.ShapeDtypeStruct((K, DS), BF16),
            jax.ShapeDtypeStruct((16, 128), F32),
            jax.ShapeDtypeStruct((DS, DS), F32),
        ),
        in_specs=[hbm] * 4,
        out_specs=(pl.BlockSpec(memory_space=pl.ANY), vmem, vmem),
        scratch_shapes=[
            pltpu.VMEM((GROUP, D), BF16),
            pltpu.VMEM((4, GROUP, DS), BF16),
            pltpu.VMEM((GROUP, DS), BF16),
            pltpu.VMEM((DS, GROUP), F32),
            pltpu.VMEM((D, DS), BF16),
            pltpu.VMEM((D, DS), BF16),
            pltpu.VMEM((16, 128), jnp.int32),
            pltpu.VMEM((4, 16, 128), jnp.int32),
            pltpu.VMEM((256, 4 * GROUP), BF16),
            pltpu.VMEM((4, GROUP, DS), BF16),
            pltpu.VMEM((5, 16, 256), F32),
            pltpu.VMEM((256, 4 * DS), F32),
            pltpu.VMEM((3, OWN, DS), BF16),
            pltpu.VMEM((3, OWN, DS), BF16),
            pltpu.VMEM((OWN, DS), F32),
            pltpu.VMEM((OWN, DS), BF16),
            pltpu.VMEM((K, DS), BF16),
            pltpu.VMEM((DS, GROUP), F32),
            pltpu.VMEM((DS, GROUP), BF16),
            pltpu.VMEM((2, 2, DS, 128), F32),
            pltpu.VMEM((3, 2, 2, DS, 128), BF16),
            pltpu.VMEM((3, 2, 2, DS, 128), BF16),
            pltpu.VMEM((3, DS, 128), BF16),
            pltpu.VMEM((3, DS, 128), BF16),
            pltpu.SemaphoreType.DMA((SEMS,)),
            pltpu.SemaphoreType.DMA((SEMS,)),
            pltpu.SemaphoreType.DMA((21,)),
        ],
        compiler_params=pltpu.CompilerParams(
            collective_id=0, has_side_effects=True, vmem_limit_bytes=48 * 1024 * 1024
        ),
        name="opq_step",
    )(*(pltpu.with_memory_space_constraint(t, pltpu.HBM) for t in operands))
    return cent.reshape(1, K, DS), dist.reshape(GROUP, 1), cross


def solution(mesh):
    placed = (P(("dp", "sub"), None), P(None, "sub"), P("sub", None, None), P("dp", "sub"))
    return jax.shard_map(
        per_device,
        mesh=mesh,
        in_specs=placed,
        out_specs=(P("sub", None, None), P("dp", "sub"), P("dp", "sub")),
        check_vma=False,
    )
```

```python
import jax
import jax.numpy as jnp
from jax import lax
from jax.experimental import pallas as pl
from jax.experimental.pallas import tpu as pltpu
from jax.sharding import PartitionSpec as P

BF16 = jnp.bfloat16
F32 = jnp.float32
MESH = pl.DeviceIdType.MESH

D = 2048
K = 4096
DS = 128
GROUP = 2048
OWN = 256
SEMS = 192


def kernel(
    v_ref, r_ref, cb_ref, codes_ref,
    cent_out, dist_ref, cross_ref,
    vg, rot, oth, rott, rown, roth, raw, codes, lo, hicol, counts, tacc, tsend, trecv, cnt, cbk, cent,
    reb, rebb, xf, xs, xr, zs, zr,
    ssem, rsem, lsem,
):
    dp = lax.axis_index("dp")
    sub = lax.axis_index("sub")
    zh, y = lax.div(dp, 4), lax.rem(dp, 4)
    x, zl, core = lax.div(sub, 4), lax.rem(lax.div(sub, 2), 2), lax.rem(sub, 2)
    xp, xm, x2 = lax.rem(x + 1, 4), lax.rem(x + 3, 4), lax.rem(x + 2, 4)
    yp, ym, y2 = lax.rem(y + 1, 4), lax.rem(y + 3, 4), lax.rem(y + 2, 4)
    zo, co = 1 - zl, 1 - core

    def sid(a, b, c):
        return a * 4 + b * 2 + c

    to_xp, to_xm = (dp, sid(xp, zl, core)), (dp, sid(xm, zl, core))
    to_z = (dp, sid(x, zo, core))
    to_core = (dp, sid(x, zl, co))
    to_out = (lax.rem(zh + 3 + 2 * zl, 4) * 4 + y, sid(x, zo, core))

    def to_y(k):
        return (zh * 4 + lax.rem(y + k, 4), sub)

    def to_zh(k):
        return (lax.rem(zh + k, 4) * 4 + y, sub)

    pending = []
    ids = {}

    def role(name):
        return ids.setdefault(name, len(ids))

    def send(name, src, dst, target):
        i = role(name)
        copy = pltpu.make_async_remote_copy(
            src_ref=src, dst_ref=dst, send_sem=ssem.at[i], recv_sem=rsem.at[i],
            device_id=target, device_id_type=MESH,
        )
        copy.start()
        pending.append(copy)

    def recv(name, ref):
        i = role(name)
        pltpu.make_async_remote_copy(
            src_ref=ref, dst_ref=ref, send_sem=ssem.at[i], recv_sem=rsem.at[i],
            device_id=to_core, device_id_type=MESH,
        ).wait_recv()

    def piece(cp, h, c):
        return pl.ds(pl.multiple_of(cp * 256 + h * 128 + c * 64, 64), 64)

    def unit(cp, h):
        return pl.ds(pl.multiple_of(cp * 256 + h * 128, 128), 128)

    def chip(cp):
        return pl.ds(pl.multiple_of(cp * 256, 256), 256)

    here, up, down, far = x * 2 + zl, xp * 2 + zl, xm * 2 + zl, x2 * 2 + zl
    here_z, up_z, down_z, far_z = x * 2 + zo, xp * 2 + zo, xm * 2 + zo, x2 * 2 + zo

    local = [
        pltpu.make_async_copy(v_ref.at[pl.ds(h * 64, 64)], vg.at[piece(here, h, core)], lsem.at[h])
        for h in range(2)
    ]
    local.append(pltpu.make_async_copy(codes_ref, raw, lsem.at[2]))
    local.append(pltpu.make_async_copy(r_ref, rown, lsem.at[3]))
    hi_own = 4 * y + zh
    own_rows = pl.ds(pl.multiple_of(hi_own * OWN, OWN), OWN)
    local.append(pltpu.make_async_copy(cb_ref.at[own_rows], cbk, lsem.at[4]))
    for copy in local:
        copy.start()

    barrier = pltpu.get_barrier_semaphore()
    peers = [to_xp, to_xm, to_z, to_core, to_out] + [to_y(k) for k in (1, 3, 2)] + [to_zh(k) for k in (1, 3, 2)]
    for peer in peers:
        pl.semaphore_signal(barrier, inc=1, device_id=peer, device_id_type=MESH)
    for copy in local:
        copy.wait()

    even, odd = raw[pl.ds(0, 8, stride=2), :], raw[pl.ds(1, 8, stride=2), :]
    first = lax.broadcasted_iota(jnp.int32, (8, 128), 1) < 64
    codes[y, 0:8, :] = jnp.where(first, even, pltpu.roll(odd, 64, 1))
    codes[y, 8:16, :] = jnp.where(first, pltpu.roll(even, 64, 1), odd)
    pl.semaphore_wait(barrier, len(peers))

    def vsend(name, cp, h, c, target):
        ref = vg.at[piece(cp, h, c)]
        send(name, ref, ref, target)

    def vrecv(name, cp, h, c):
        recv(name, vg.at[piece(cp, h, c)])

    vsend("xm0", here, 0, core, to_xp)
    vsend("xp0", here, 0, core, to_xm)
    top, low = pl.ds(0, 1024), pl.ds(1024, 1024)
    send("r_in", rown.at[top], roth.at[top], to_z)
    send("r_out", rown.at[low], roth.at[low], to_out)
    for h in range(2):
        vsend("d_own%d" % h, here, h, core, to_core)
    for k in (1, 3, 2):
        send("code%d" % k, codes.at[y], codes.at[y], to_y(k))
    vsend("xm1", here, 1, core, to_xp)
    vsend("xp1", here, 1, core, to_xm)

    def quarter(cp, h, v, c):
        return vg.at[pl.ds(pl.multiple_of(cp * 256 + h * 128 + c * 64 + v * 32, 32), 32)]

    def x_forward(h):
        vrecv("xm%d" % h, down, h, core)
        ref = quarter(down, h, 0, core)
        send("xf%d" % h, ref, ref, to_xp)
        vsend("d_xm%d" % h, down, h, core, to_core)
        vrecv("xp%d" % h, up, h, core)
        ref = quarter(up, h, 1, core)
        send("xg%d" % h, ref, ref, to_xm)
        vsend("d_xp%d" % h, up, h, core, to_core)

    def x_far(h):
        recv("xf%d" % h, quarter(far, h, 0, core))
        recv("xg%d" % h, quarter(far, h, 1, core))
        vsend("d_x2%d" % h, far, h, core, to_core)
        vrecv("d_x2%d" % h, far, h, co)

    def y_send(name, rows, direct):
        ref = rot.at[y, rows]
        send("a" + name, ref, ref, to_y(1))
        send("b" + name, ref, ref, to_y(3))
        if direct:
            send("c" + name, ref, ref, to_y(2))

    def halves(start, size):
        a = pl.ds(pl.multiple_of(start, 64), size)
        b = pl.ds(pl.multiple_of(start + size, 64), size)
        return a, b

    def y_forward(name, start, size):
        rows = pl.ds(pl.multiple_of(start, 128), size)
        a, b = halves(start, size // 2)
        recv("a" + name, rot.at[ym, rows])
        ref = rot.at[ym, a]
        send("c" + name, ref, ref, to_y(1))
        recv("b" + name, rot.at[yp, rows])
        ref = rot.at[yp, b]
        send("d" + name, ref, ref, to_y(3))

    def y_last(name, start, size, direct):
        if direct:
            rows = pl.ds(pl.multiple_of(start, 128), size)
            recv("a" + name, rot.at[ym, rows])
            recv("b" + name, rot.at[yp, rows])
            recv("c" + name, rot.at[y2, rows])
        else:
            a, b = halves(start, size // 2)
            recv("c" + name, rot.at[y2, a])
            recv("d" + name, rot.at[y2, b])

    def rot_own(rows):
        part = jnp.dot(vg[rows, :], rown[...], preferred_element_type=F32)
        rot[y, rows, :] = part.astype(BF16)

    def rot_oth(rows):
        part = jnp.dot(vg[rows, :], roth[...], preferred_element_type=F32)
        oth[rows, :] = part.astype(BF16)

    def rot_both(rows):
        both = jnp.concatenate([rown[...], roth[...]], axis=1)
        part = jnp.dot(vg[rows, :], both, preferred_element_type=F32)
        rot[y, rows, :] = part[:, :DS].astype(BF16)
        oth[rows, :] = part[:, DS:].astype(BF16)

    def z_send(name, rows):
        send("z" + name, oth.at[rows], rot.at[y, rows], to_z)

    def z_recv(name, rows):
        recv("z" + name, rot.at[y, rows])

    for h in range(2):
        vrecv("d_own%d" % h, here, h, co)
    rot_own(chip(here))
    y_send("A", chip(here), False)

    for k in (1, 3, 2):
        recv("code%d" % k, codes.at[lax.rem(y + 4 - k, 4)])
    tacc[...] = jnp.zeros_like(tacc)
    iota = lax.broadcasted_iota(jnp.int32, (256, 128), 0)

    def lo_table(g, carry):
        tile = jnp.bitwise_and(codes[g], 255)
        for i in range(16):
            cp, h = i // 2, i % 2
            row = tile[h * 8 + cp:h * 8 + cp + 1, :]
            mark = jnp.where(iota == jnp.broadcast_to(row, (256, 128)), 1.0, 0.0)
            lo[:, pl.ds(pl.multiple_of(g * GROUP + i * 128, 128), 128)] = mark.astype(BF16)
        return carry

    lax.fori_loop(0, 4, lo_table, 0)

    def hi_table(g, carry):
        tile = lax.shift_right_logical(codes[g], 8).astype(F32)
        for i in range(16):
            cp, h = i // 2, i % 2
            row = tile[h * 8 + cp:h * 8 + cp + 1, :]
            hicol[g, i * 128:(i + 1) * 128, :] = jnp.broadcast_to(row, (128, 128)).T.astype(BF16)
        return carry

    x_forward(0)
    recv("r_in", roth.at[top])
    recv("r_out", roth.at[low])
    rot_oth(chip(here))
    z_send("A", chip(here))
    vrecv("d_xm0", down, 0, co)
    rot_both(unit(down, 0))
    y_send("B", unit(down, 0), False)
    z_send("B", unit(down, 0))
    vrecv("d_xp0", up, 0, co)
    rot_both(unit(up, 0))
    y_send("C", unit(up, 0), False)
    z_send("C", unit(up, 0))
    vsend("w0", here, 0, core, to_z)
    y_forward("A", here * 256, 256)
    lax.fori_loop(0, 4, hi_table, 0)

    z_recv("A", chip(here_z))
    y_send("Az", chip(here_z), False)
    z_recv("B", unit(down_z, 0))
    y_send("Bz", unit(down_z, 0), False)
    z_recv("C", unit(up_z, 0))
    y_send("Cz", unit(up_z, 0), False)
    y_forward("B", down * 256, 128)
    y_forward("C", up * 256, 128)

    def count(g, acc):
        for h in range(2):
            for cp in range(8):
                row = lax.shift_right_logical(codes[g, h * 8 + cp:h * 8 + cp + 1, :], 8)
                mark = jnp.where(iota[:16] == jnp.broadcast_to(row, (16, 128)), 1.0, 0.0).astype(BF16)
                tab = lo[:, pl.ds(pl.multiple_of(g * GROUP + (cp * 2 + h) * 128, 128), 128)]
                acc = acc + lax.dot_general(mark, tab, (((1,), (1,)), ((), ())), preferred_element_type=F32)
        return acc

    counts[0] = lax.fori_loop(0, 4, count, jnp.zeros((16, 256), F32))
    for k in (1, 3, 2):
        send("n%d" % k, counts.at[0], counts.at[k], to_zh(k))

    x_forward(1)
    vrecv("d_xm1", down, 1, co)
    rot_both(unit(down, 1))
    y_send("D", unit(down, 1), False)
    z_send("D", unit(down, 1))
    vrecv("d_xp1", up, 1, co)
    rot_both(unit(up, 1))
    y_send("E", unit(up, 1), False)
    z_send("E", unit(up, 1))
    y_forward("Az", here_z * 256, 256)
    y_forward("Bz", down_z * 256, 128)
    y_forward("Cz", up_z * 256, 128)

    def accumulate(cp):
        marks, wides = [], []
        for g in range(4):
            marks.append(lo[:, pl.ds(pl.multiple_of(g * GROUP + cp * 256, 256), 256)])
            values = rot[g, chip(cp), :]
            his = hicol[g, chip(cp), :]
            parts = []
            for h in range(4):
                want = (4 * y + h).astype(F32).astype(BF16)
                parts.append(jnp.where(his == want, values, jnp.zeros_like(values)))
            wides.append(jnp.concatenate(parts, axis=1))
        mark, wide = jnp.concatenate(marks, axis=1), jnp.concatenate(wides, axis=0)
        tacc[...] += jnp.dot(mark, wide, preferred_element_type=F32)

    y_last("A", here * 256, 256, False)
    accumulate(here)
    x_far(0)
    rot_both(unit(far, 0))
    z_send("F", unit(far, 0))
    y_send("F", unit(far, 0), True)
    z_recv("D", unit(down_z, 1))
    y_send("Dz", unit(down_z, 1), False)
    z_recv("E", unit(up_z, 1))
    y_send("Ez", unit(up_z, 1), False)
    y_forward("D", down * 256 + 128, 128)
    y_forward("E", up * 256 + 128, 128)

    x_far(1)
    rot_both(unit(far, 1))
    z_send("G", unit(far, 1))
    y_send("G", unit(far, 1), True)
    vsend("w1", here, 1, core, to_z)
    vrecv("w0", here_z, 0, core)
    vsend("wm0", here_z, 0, core, to_xp)
    vsend("wp0", here_z, 0, core, to_xm)
    vsend("d_w0", here_z, 0, core, to_core)
    z_recv("F", unit(far_z, 0))
    y_send("Fz", unit(far_z, 0), True)
    y_forward("Dz", down_z * 256 + 128, 128)
    y_forward("Ez", up_z * 256 + 128, 128)
    z_recv("G", unit(far_z, 1))
    y_send("Gz", unit(far_z, 1), True)
    y_last("Az", here_z * 256, 256, False)
    accumulate(here_z)
    y_last("B", down * 256, 128, False)
    y_last("D", down * 256 + 128, 128, False)
    accumulate(down)
    y_last("C", up * 256, 128, False)
    y_last("E", up * 256 + 128, 128, False)
    accumulate(up)
    y_last("Bz", down_z * 256, 128, False)
    y_last("Dz", down_z * 256 + 128, 128, False)
    accumulate(down_z)
    y_last("Cz", up_z * 256, 128, False)
    y_last("Ez", up_z * 256 + 128, 128, False)
    accumulate(up_z)
    vrecv("w1", here_z, 1, core)
    vsend("wp1", here_z, 1, core, to_xm)
    vsend("wm1", here_z, 1, core, to_xp)
    vsend("d_w1", here_z, 1, core, to_core)
    vrecv("wm0", down_z, 0, core)
    vsend("w20", down_z, 0, core, to_xp)
    vsend("d_wm0", down_z, 0, core, to_core)
    vrecv("wp0", up_z, 0, core)
    vsend("d_wp0", up_z, 0, core, to_core)
    y_last("F", far * 256, 128, True)
    y_last("G", far * 256 + 128, 128, True)
    accumulate(far)
    y_last("Fz", far_z * 256, 128, True)
    y_last("Gz", far_z * 256 + 128, 128, True)
    accumulate(far_z)

    def part(hb):
        return pl.ds(hb * 128, 128)

    for hb in range(2):
        for k in (2, 1, 3):
            theirs = pl.ds(pl.multiple_of(lax.rem(zh + k, 4) * DS, DS), DS)
            tsend[k - 1, part(hb), :] = tacc[part(hb), theirs].astype(BF16)
            send("t%d%d" % (k, hb), tsend.at[k - 1, part(hb)], trecv.at[k - 1, part(hb)], to_zh(k))
    for k in (1, 3, 2):
        recv("n%d" % k, counts.at[k])
    counts[4] = counts[0] + counts[1] + counts[2] + counts[3]
    mine = counts[4, pl.ds(hi_own, 1), :]
    cnt[...] = jnp.broadcast_to(mine, (128, 256)).T
    rott[...] = rot[y].astype(F32).T
    vrecv("wp1", up_z, 1, core)
    vsend("w21", up_z, 1, core, to_xm)
    vsend("d_wp1", up_z, 1, core, to_core)
    vrecv("wm1", down_z, 1, core)
    vsend("d_wm1", down_z, 1, core, to_core)

    def chunk(a, b):
        return pl.ds(pl.multiple_of(b * 1024 + a * OWN, OWN), OWN)

    def half_chunk(a, b, hb):
        return pl.ds(pl.multiple_of(b * 1024 + a * OWN + hb * 128, 128), 128)

    def quarter_chunk(a, b, hb, v):
        return pl.ds(pl.multiple_of(b * 1024 + a * OWN + hb * 128 + v * 64, 64), 64)

    def y_chunk_send(q, hb):
        ref = cent.at[half_chunk(zs_of[q], y, hb)]
        send("ca%d%d" % (q, hb), ref, ref, to_y(1))
        send("cb%d%d" % (q, hb), ref, ref, to_y(3))

    def y_chunk_forward(q, hb):
        a = zs_of[q]
        recv("ca%d%d" % (q, hb), cent.at[half_chunk(a, ym, hb)])
        ref = cent.at[quarter_chunk(a, ym, hb, 0)]
        send("cc%d%d" % (q, hb), ref, ref, to_y(1))
        recv("cb%d%d" % (q, hb), cent.at[half_chunk(a, yp, hb)])
        ref = cent.at[quarter_chunk(a, yp, hb, 1)]
        send("cd%d%d" % (q, hb), ref, ref, to_y(3))

    def z_chunk(q, hb):
        recv("cz%d%d" % (q, hb), cent.at[half_chunk(zs_of[q], y, hb)])
        y_chunk_send(q, hb)

    zs_of = [zh] + [lax.rem(zh + 4 - q, 4) for q in (1, 2, 3)]
    for hb in range(2):
        total = tacc[part(hb), pl.ds(pl.multiple_of(zh * DS, DS), DS)]
        for k in (1, 3, 2):
            recv("t%d%d" % (k, hb), trecv.at[k - 1, part(hb)])
            total = total + trecv[k - 1, part(hb), :].astype(F32)
        value = (total + cbk[part(hb), :].astype(F32)) / (cnt[part(hb), :] + 1.0)
        cent[half_chunk(zh, y, hb), :] = value.astype(BF16)
        ref = cent.at[half_chunk(zh, y, hb)]
        for k in (1, 3, 2):
            send("cz%d%d" % (k, hb), ref, ref, to_zh(k))
        y_chunk_send(0, hb)

    outs = []

    def rebuild(a, b):
        copy = pltpu.make_async_copy(
            cent.at[chunk(a, b)], cent_out.at[chunk(a, b)], lsem.at[5 + len(outs)]
        )
        copy.start()
        outs.append(copy)
        table = cent[chunk(a, b), :].astype(F32).T.astype(BF16)
        want = 4 * b + a
        for i in range(8):
            tab = lo[:, pl.ds(pl.multiple_of(y * GROUP + i * 256, 256), 256)]
            got = jnp.dot(table, tab, preferred_element_type=F32)
            place = slice(i * 256, (i + 1) * 256)
            row = jnp.concatenate([codes[y, i:i + 1, :], codes[y, i + 8:i + 9, :]], axis=1)
            hit = lax.shift_right_logical(row, 8) == want
            reb[:, place] = jnp.where(jnp.broadcast_to(hit, (128, 256)), got, reb[:, place])

    reb[...] = jnp.zeros_like(reb)
    y_chunk_forward(0, 0)
    z_chunk(1, 0)
    z_chunk(3, 0)
    y_chunk_forward(0, 1)
    rebuild(zh, y)
    z_chunk(2, 0)
    y_chunk_forward(1, 0)
    y_chunk_forward(3, 0)
    rebuild(zh, ym)
    rebuild(zh, yp)
    z_chunk(1, 1)
    z_chunk(3, 1)
    y_chunk_forward(2, 0)
    z_chunk(2, 1)
    vrecv("w20", far_z, 0, core)
    vsend("d_w20", far_z, 0, core, to_core)
    vrecv("w21", far_z, 1, core)
    vsend("d_w21", far_z, 1, core, to_core)
    rebuild(zs_of[1], y)
    rebuild(zs_of[3], y)
    y_chunk_forward(1, 1)
    y_chunk_forward(3, 1)
    rebuild(zs_of[2], y)
    y_chunk_forward(2, 1)
    for q in (1, 3, 2):
        rebuild(zs_of[q], ym)
        rebuild(zs_of[q], yp)

    for q in (0, 1, 3, 2):
        a = zs_of[q]
        for hb in range(2):
            recv("cc%d%d" % (q, hb), cent.at[quarter_chunk(a, y2, hb, 0)])
            recv("cd%d%d" % (q, hb), cent.at[quarter_chunk(a, y2, hb, 1)])
        rebuild(a, y2)
    for h in range(2):
        vrecv("d_w%d" % h, here_z, h, co)
        vrecv("d_wm%d" % h, down_z, h, co)
        vrecv("d_wp%d" % h, up_z, h, co)
        vrecv("d_w2%d" % h, far_z, h, co)

    rebb[...] = reb[...].astype(BF16)

    pairs = ((2, 1), (3, 0))

    def cross_part(k, p):
        to = lax.rem(y + k, 4)
        blocks = []
        for z in pairs[p]:
            column = (lax.rem(zh + z, 4) * 4 + to) * 128
            blocks.append(vg[:, pl.ds(pl.multiple_of(column, 128), 128)])
        got = jnp.dot(rebb[...], jnp.concatenate(blocks, axis=1), preferred_element_type=F32)
        if k == 0:
            xf[p, 0] = got[:, :128]
            xf[p, 1] = got[:, 128:]
        else:
            xs[k - 1, p, 0] = got[:, :128].astype(BF16)
            xs[k - 1, p, 1] = got[:, 128:].astype(BF16)
            send("xa%d%d" % (k, p), xs.at[k - 1, p], xr.at[k - 1, p], to_y(k))

    for p in range(2):
        for k in (2, 1, 3):
            cross_part(k, p)
    for p in range(2):
        cross_part(0, p)

    gap = rott[...] - reb[...]
    gap = jnp.sum(gap * gap, axis=0, keepdims=True)
    half_row = lax.broadcasted_iota(jnp.int32, (1, 128), 1) < 64
    for cp in range(8):
        u0, u1 = gap[:, cp * 256:cp * 256 + 128], gap[:, cp * 256 + 128:cp * 256 + 256]
        dist_ref[2 * cp:2 * cp + 1, :] = jnp.where(half_row, u0, pltpu.roll(u1, 64, 1))
        dist_ref[2 * cp + 1:2 * cp + 2, :] = jnp.where(half_row, pltpu.roll(u0, 64, 1), u1)

    def cross_sum(p):
        for k in (1, 3, 2):
            recv("xa%d%d" % (k, p), xr.at[k - 1, p])
        return [xf[p, i] + xr[0, p, i].astype(F32) + xr[1, p, i].astype(F32) + xr[2, p, i].astype(F32) for i in range(2)]

    def cross_zh(k, value):
        zs[k - 1] = value.astype(BF16)
        send("xz%d" % k, zs.at[k - 1], zr.at[k - 1], to_zh(k))

    two, one = cross_sum(0)
    cross_zh(2, two)
    cross_zh(1, one)
    three, out = cross_sum(1)
    cross_zh(3, three)
    for k in (1, 2, 3):
        recv("xz%d" % k, zr.at[k - 1])
        out = out + zr[k - 1].astype(F32)
    cross_ref[...] = out.T

    for copy in outs:
        copy.wait()
    for copy in pending:
        copy.wait_send()


def hand_out(a_ref, b_ref, c_ref, a_out, b_out, c_out, sem):
    copies = [
        pltpu.make_async_copy(src, dst, sem.at[i])
        for i, (src, dst) in enumerate(((a_ref, a_out), (b_ref, b_out), (c_ref, c_out)))
    ]
    for copy in copies:
        copy.start()
    for copy in copies:
        copy.wait()


def per_device(vectors, rotation, codebook, codes):
    vmem = pl.BlockSpec(memory_space=pltpu.VMEM)
    hbm = pl.BlockSpec(memory_space=pltpu.HBM)
    operands = (vectors, rotation, codebook.reshape(K, DS), codes.reshape(16, 128))
    cent, dist, cross = pl.pallas_call(
        kernel,
        out_shape=(
            jax.ShapeDtypeStruct((K, DS), BF16),
            jax.ShapeDtypeStruct((16, 128), F32),
            jax.ShapeDtypeStruct((DS, DS), F32),
        ),
        in_specs=[hbm] * 4,
        out_specs=(pl.BlockSpec(memory_space=pl.ANY), vmem, vmem),
        scratch_shapes=[
            pltpu.VMEM((GROUP, D), BF16),
            pltpu.VMEM((4, GROUP, DS), BF16),
            pltpu.VMEM((GROUP, DS), BF16),
            pltpu.VMEM((DS, GROUP), F32),
            pltpu.VMEM((D, DS), BF16),
            pltpu.VMEM((D, DS), BF16),
            pltpu.VMEM((16, 128), jnp.int32),
            pltpu.VMEM((4, 16, 128), jnp.int32),
            pltpu.VMEM((256, 4 * GROUP), BF16),
            pltpu.VMEM((4, GROUP, DS), BF16),
            pltpu.VMEM((5, 16, 256), F32),
            pltpu.VMEM((256, 4 * DS), F32),
            pltpu.VMEM((3, OWN, DS), BF16),
            pltpu.VMEM((3, OWN, DS), BF16),
            pltpu.VMEM((OWN, DS), F32),
            pltpu.VMEM((OWN, DS), BF16),
            pltpu.VMEM((K, DS), BF16),
            pltpu.VMEM((DS, GROUP), F32),
            pltpu.VMEM((DS, GROUP), BF16),
            pltpu.VMEM((2, 2, DS, 128), F32),
            pltpu.VMEM((3, 2, 2, DS, 128), BF16),
            pltpu.VMEM((3, 2, 2, DS, 128), BF16),
            pltpu.VMEM((3, DS, 128), BF16),
            pltpu.VMEM((3, DS, 128), BF16),
            pltpu.SemaphoreType.DMA((SEMS,)),
            pltpu.SemaphoreType.DMA((SEMS,)),
            pltpu.SemaphoreType.DMA((21,)),
        ],
        compiler_params=pltpu.CompilerParams(
            collective_id=0, has_side_effects=True, vmem_limit_bytes=48 * 1024 * 1024
        ),
        name="opq_step",
    )(*(pltpu.with_memory_space_constraint(t, pltpu.HBM) for t in operands))
    whole = pl.BlockSpec(memory_space=pl.ANY)
    cent, dist, cross = pl.pallas_call(
        hand_out,
        out_shape=tuple(jax.ShapeDtypeStruct(t.shape, t.dtype) for t in (cent, dist, cross)),
        in_specs=[whole] * 3,
        out_specs=(whole,) * 3,
        scratch_shapes=[pltpu.SemaphoreType.DMA((3,))],
        compiler_params=pltpu.CompilerParams(vmem_limit_bytes=4 * 1024 * 1024),
        name="hand_out",
    )(cent, dist, cross)
    return cent.reshape(1, K, DS), dist.reshape(GROUP, 1), cross


def solution(mesh):
    placed = (P(("dp", "sub"), None), P(None, "sub"), P("sub", None, None), P("dp", "sub"))
    return jax.shard_map(
        per_device,
        mesh=mesh,
        in_specs=placed,
        out_specs=(P("sub", None, None), P("dp", "sub"), P("dp", "sub")),
        check_vma=False,
    )
```

```python
import jax
import jax.numpy as jnp
from jax import lax
from jax.experimental import pallas as pl
from jax.experimental.pallas import tpu as pltpu
from jax.sharding import PartitionSpec as P

BF16 = jnp.bfloat16
F32 = jnp.float32
MESH = pl.DeviceIdType.MESH

D = 2048
K = 4096
DS = 128
GROUP = 2048
OWN = 256
SEMS = 192


def kernel(
    v_ref, r_ref, cb_ref, codes_ref,
    cent_out, dist_ref, cross_ref,
    vg, rot, oth, rott, rown, roth, raw, codes, lo, hicol, counts, tacc, tsend, trecv, cnt, cbk, cent,
    reb, rebb, xf, xs, xr, zs, zr,
    ssem, rsem, lsem,
):
    dp = lax.axis_index("dp")
    sub = lax.axis_index("sub")
    zh, y = lax.div(dp, 4), lax.rem(dp, 4)
    x, zl, core = lax.div(sub, 4), lax.rem(lax.div(sub, 2), 2), lax.rem(sub, 2)
    xp, xm, x2 = lax.rem(x + 1, 4), lax.rem(x + 3, 4), lax.rem(x + 2, 4)
    yp, ym, y2 = lax.rem(y + 1, 4), lax.rem(y + 3, 4), lax.rem(y + 2, 4)
    zo, co = 1 - zl, 1 - core

    def sid(a, b, c):
        return a * 4 + b * 2 + c

    to_xp, to_xm = (dp, sid(xp, zl, core)), (dp, sid(xm, zl, core))
    to_z = (dp, sid(x, zo, core))
    to_core = (dp, sid(x, zl, co))
    to_out = (lax.rem(zh + 3 + 2 * zl, 4) * 4 + y, sid(x, zo, core))

    def to_y(k):
        return (zh * 4 + lax.rem(y + k, 4), sub)

    def to_zh(k):
        return (lax.rem(zh + k, 4) * 4 + y, sub)

    pending = []
    ids = {}

    def role(name):
        return ids.setdefault(name, len(ids))

    def send(name, src, dst, target):
        i = role(name)
        copy = pltpu.make_async_remote_copy(
            src_ref=src, dst_ref=dst, send_sem=ssem.at[i], recv_sem=rsem.at[i],
            device_id=target, device_id_type=MESH,
        )
        copy.start()
        pending.append(copy)

    def recv(name, ref):
        i = role(name)
        pltpu.make_async_remote_copy(
            src_ref=ref, dst_ref=ref, send_sem=ssem.at[i], recv_sem=rsem.at[i],
            device_id=to_core, device_id_type=MESH,
        ).wait_recv()

    def piece(cp, h, c):
        return pl.ds(pl.multiple_of(cp * 256 + h * 128 + c * 64, 64), 64)

    def unit(cp, h):
        return pl.ds(pl.multiple_of(cp * 256 + h * 128, 128), 128)

    def chip(cp):
        return pl.ds(pl.multiple_of(cp * 256, 256), 256)

    here, up, down, far = x * 2 + zl, xp * 2 + zl, xm * 2 + zl, x2 * 2 + zl
    here_z, up_z, down_z, far_z = x * 2 + zo, xp * 2 + zo, xm * 2 + zo, x2 * 2 + zo

    local = [
        pltpu.make_async_copy(v_ref.at[pl.ds(h * 64, 64)], vg.at[piece(here, h, core)], lsem.at[h])
        for h in range(2)
    ]
    local.append(pltpu.make_async_copy(codes_ref, raw, lsem.at[2]))
    local.append(pltpu.make_async_copy(r_ref, rown, lsem.at[3]))
    hi_own = 4 * y + zh
    own_rows = pl.ds(pl.multiple_of(hi_own * OWN, OWN), OWN)
    local.append(pltpu.make_async_copy(cb_ref.at[own_rows], cbk, lsem.at[4]))
    for copy in local:
        copy.start()

    barrier = pltpu.get_barrier_semaphore()
    peers = [to_xp, to_xm, to_z, to_core, to_out] + [to_y(k) for k in (1, 3, 2)] + [to_zh(k) for k in (1, 3, 2)]
    for peer in peers:
        pl.semaphore_signal(barrier, inc=1, device_id=peer, device_id_type=MESH)
    for copy in local:
        copy.wait()

    even, odd = raw[pl.ds(0, 8, stride=2), :], raw[pl.ds(1, 8, stride=2), :]
    first = lax.broadcasted_iota(jnp.int32, (8, 128), 1) < 64
    codes[y, 0:8, :] = jnp.where(first, even, pltpu.roll(odd, 64, 1))
    codes[y, 8:16, :] = jnp.where(first, pltpu.roll(even, 64, 1), odd)
    pl.semaphore_wait(barrier, len(peers))

    def vsend(name, cp, h, c, target):
        ref = vg.at[piece(cp, h, c)]
        send(name, ref, ref, target)

    def vrecv(name, cp, h, c):
        recv(name, vg.at[piece(cp, h, c)])

    vsend("xm0", here, 0, core, to_xp)
    vsend("xp0", here, 0, core, to_xm)
    top, low = pl.ds(0, 1024), pl.ds(1024, 1024)
    send("r_in", rown.at[top], roth.at[top], to_z)
    send("r_out", rown.at[low], roth.at[low], to_out)
    for h in range(2):
        vsend("d_own%d" % h, here, h, core, to_core)
    for k in (1, 3, 2):
        send("code%d" % k, codes.at[y], codes.at[y], to_y(k))
    vsend("xm1", here, 1, core, to_xp)
    vsend("xp1", here, 1, core, to_xm)

    def quarter(cp, h, v, c):
        return vg.at[pl.ds(pl.multiple_of(cp * 256 + h * 128 + c * 64 + v * 32, 32), 32)]

    def x_forward(h):
        vrecv("xm%d" % h, down, h, core)
        ref = quarter(down, h, 0, core)
        send("xf%d" % h, ref, ref, to_xp)
        vsend("d_xm%d" % h, down, h, core, to_core)
        vrecv("xp%d" % h, up, h, core)
        ref = quarter(up, h, 1, core)
        send("xg%d" % h, ref, ref, to_xm)
        vsend("d_xp%d" % h, up, h, core, to_core)

    def x_far(h):
        recv("xf%d" % h, quarter(far, h, 0, core))
        recv("xg%d" % h, quarter(far, h, 1, core))
        vsend("d_x2%d" % h, far, h, core, to_core)
        vrecv("d_x2%d" % h, far, h, co)

    def y_send(name, rows, direct):
        ref = rot.at[y, rows]
        send("a" + name, ref, ref, to_y(1))
        send("b" + name, ref, ref, to_y(3))
        if direct:
            send("c" + name, ref, ref, to_y(2))

    def halves(start, size):
        a = pl.ds(pl.multiple_of(start, 64), size)
        b = pl.ds(pl.multiple_of(start + size, 64), size)
        return a, b

    def y_forward(name, start, size):
        rows = pl.ds(pl.multiple_of(start, 128), size)
        a, b = halves(start, size // 2)
        recv("a" + name, rot.at[ym, rows])
        ref = rot.at[ym, a]
        send("c" + name, ref, ref, to_y(1))
        recv("b" + name, rot.at[yp, rows])
        ref = rot.at[yp, b]
        send("d" + name, ref, ref, to_y(3))

    def y_last(name, start, size, direct):
        if direct:
            rows = pl.ds(pl.multiple_of(start, 128), size)
            recv("a" + name, rot.at[ym, rows])
            recv("b" + name, rot.at[yp, rows])
            recv("c" + name, rot.at[y2, rows])
        else:
            a, b = halves(start, size // 2)
            recv("c" + name, rot.at[y2, a])
            recv("d" + name, rot.at[y2, b])

    def rot_own(rows):
        part = jnp.dot(vg[rows, :], rown[...], preferred_element_type=F32)
        rot[y, rows, :] = part.astype(BF16)

    def rot_oth(rows):
        part = jnp.dot(vg[rows, :], roth[...], preferred_element_type=F32)
        oth[rows, :] = part.astype(BF16)

    def rot_both(rows):
        both = jnp.concatenate([rown[...], roth[...]], axis=1)
        part = jnp.dot(vg[rows, :], both, preferred_element_type=F32)
        rot[y, rows, :] = part[:, :DS].astype(BF16)
        oth[rows, :] = part[:, DS:].astype(BF16)

    def z_send(name, rows):
        send("z" + name, oth.at[rows], rot.at[y, rows], to_z)

    def z_recv(name, rows):
        recv("z" + name, rot.at[y, rows])

    for h in range(2):
        vrecv("d_own%d" % h, here, h, co)
    rot_own(chip(here))
    y_send("A", chip(here), False)

    for k in (1, 3, 2):
        recv("code%d" % k, codes.at[lax.rem(y + 4 - k, 4)])
    tacc[...] = jnp.zeros_like(tacc)
    iota = lax.broadcasted_iota(jnp.int32, (256, 128), 0)

    def lo_table(g, carry):
        tile = jnp.bitwise_and(codes[g], 255)
        for i in range(16):
            cp, h = i // 2, i % 2
            row = tile[h * 8 + cp:h * 8 + cp + 1, :]
            mark = jnp.where(iota == jnp.broadcast_to(row, (256, 128)), 1.0, 0.0)
            lo[:, pl.ds(pl.multiple_of(g * GROUP + i * 128, 128), 128)] = mark.astype(BF16)
        return carry

    lax.fori_loop(0, 4, lo_table, 0)

    def hi_table(g, carry):
        tile = lax.shift_right_logical(codes[g], 8).astype(F32)
        for i in range(16):
            cp, h = i // 2, i % 2
            row = tile[h * 8 + cp:h * 8 + cp + 1, :]
            hicol[g, i * 128:(i + 1) * 128, :] = jnp.broadcast_to(row, (128, 128)).T.astype(BF16)
        return carry

    x_forward(0)
    recv("r_in", roth.at[top])
    recv("r_out", roth.at[low])
    rot_oth(chip(here))
    z_send("A", chip(here))
    vrecv("d_xm0", down, 0, co)
    rot_both(unit(down, 0))
    y_send("B", unit(down, 0), False)
    z_send("B", unit(down, 0))
    vrecv("d_xp0", up, 0, co)
    rot_both(unit(up, 0))
    y_send("C", unit(up, 0), False)
    z_send("C", unit(up, 0))
    vsend("w0", here, 0, core, to_z)
    y_forward("A", here * 256, 256)
    lax.fori_loop(0, 4, hi_table, 0)

    z_recv("A", chip(here_z))
    y_send("Az", chip(here_z), False)
    z_recv("B", unit(down_z, 0))
    y_send("Bz", unit(down_z, 0), False)
    z_recv("C", unit(up_z, 0))
    y_send("Cz", unit(up_z, 0), False)
    y_forward("B", down * 256, 128)
    y_forward("C", up * 256, 128)

    def count(g, acc):
        for h in range(2):
            for cp in range(8):
                row = lax.shift_right_logical(codes[g, h * 8 + cp:h * 8 + cp + 1, :], 8)
                mark = jnp.where(iota[:16] == jnp.broadcast_to(row, (16, 128)), 1.0, 0.0).astype(BF16)
                tab = lo[:, pl.ds(pl.multiple_of(g * GROUP + (cp * 2 + h) * 128, 128), 128)]
                acc = acc + lax.dot_general(mark, tab, (((1,), (1,)), ((), ())), preferred_element_type=F32)
        return acc

    counts[0] = lax.fori_loop(0, 4, count, jnp.zeros((16, 256), F32))
    for k in (1, 3, 2):
        send("n%d" % k, counts.at[0], counts.at[k], to_zh(k))

    x_forward(1)
    vrecv("d_xm1", down, 1, co)
    rot_both(unit(down, 1))
    y_send("D", unit(down, 1), False)
    z_send("D", unit(down, 1))
    vrecv("d_xp1", up, 1, co)
    rot_both(unit(up, 1))
    y_send("E", unit(up, 1), False)
    z_send("E", unit(up, 1))
    y_forward("Az", here_z * 256, 256)
    y_forward("Bz", down_z * 256, 128)
    y_forward("Cz", up_z * 256, 128)

    def accumulate(cp):
        marks, wides = [], []
        for g in range(4):
            marks.append(lo[:, pl.ds(pl.multiple_of(g * GROUP + cp * 256, 256), 256)])
            values = rot[g, chip(cp), :]
            his = hicol[g, chip(cp), :]
            parts = []
            for h in range(4):
                want = (4 * y + h).astype(F32).astype(BF16)
                parts.append(jnp.where(his == want, values, jnp.zeros_like(values)))
            wides.append(jnp.concatenate(parts, axis=1))
        mark, wide = jnp.concatenate(marks, axis=1), jnp.concatenate(wides, axis=0)
        tacc[...] += jnp.dot(mark, wide, preferred_element_type=F32)

    y_last("A", here * 256, 256, False)
    accumulate(here)
    x_far(0)
    rot_both(unit(far, 0))
    z_send("F", unit(far, 0))
    y_send("F", unit(far, 0), True)
    z_recv("D", unit(down_z, 1))
    y_send("Dz", unit(down_z, 1), False)
    z_recv("E", unit(up_z, 1))
    y_send("Ez", unit(up_z, 1), False)
    y_forward("D", down * 256 + 128, 128)
    y_forward("E", up * 256 + 128, 128)

    x_far(1)
    rot_both(unit(far, 1))
    z_send("G", unit(far, 1))
    y_send("G", unit(far, 1), True)
    vsend("w1", here, 1, core, to_z)
    vrecv("w0", here_z, 0, core)
    vsend("wm0", here_z, 0, core, to_xp)
    vsend("wp0", here_z, 0, core, to_xm)
    vsend("d_w0", here_z, 0, core, to_core)
    z_recv("F", unit(far_z, 0))
    y_send("Fz", unit(far_z, 0), True)
    y_forward("Dz", down_z * 256 + 128, 128)
    y_forward("Ez", up_z * 256 + 128, 128)
    z_recv("G", unit(far_z, 1))
    y_send("Gz", unit(far_z, 1), True)
    y_last("Az", here_z * 256, 256, False)
    accumulate(here_z)
    y_last("B", down * 256, 128, False)
    y_last("D", down * 256 + 128, 128, False)
    accumulate(down)
    y_last("C", up * 256, 128, False)
    y_last("E", up * 256 + 128, 128, False)
    accumulate(up)
    y_last("Bz", down_z * 256, 128, False)
    y_last("Dz", down_z * 256 + 128, 128, False)
    accumulate(down_z)
    y_last("Cz", up_z * 256, 128, False)
    y_last("Ez", up_z * 256 + 128, 128, False)
    accumulate(up_z)
    y_last("F", far * 256, 128, True)
    y_last("G", far * 256 + 128, 128, True)
    accumulate(far)
    y_last("Fz", far_z * 256, 128, True)
    y_last("Gz", far_z * 256 + 128, 128, True)
    accumulate(far_z)

    def part(hb):
        return pl.ds(hb * 128, 128)

    for hb in range(2):
        for k in (2, 1, 3):
            theirs = pl.ds(pl.multiple_of(lax.rem(zh + k, 4) * DS, DS), DS)
            tsend[k - 1, part(hb), :] = tacc[part(hb), theirs].astype(BF16)
            send("t%d%d" % (k, hb), tsend.at[k - 1, part(hb)], trecv.at[k - 1, part(hb)], to_zh(k))
    vrecv("w1", here_z, 1, core)
    vsend("wp1", here_z, 1, core, to_xm)
    vsend("wm1", here_z, 1, core, to_xp)
    vsend("d_w1", here_z, 1, core, to_core)
    vrecv("wm0", down_z, 0, core)
    vsend("w20", down_z, 0, core, to_xp)
    vsend("d_wm0", down_z, 0, core, to_core)
    vrecv("wp0", up_z, 0, core)
    vsend("d_wp0", up_z, 0, core, to_core)
    for k in (1, 3, 2):
        recv("n%d" % k, counts.at[k])
    counts[4] = counts[0] + counts[1] + counts[2] + counts[3]
    mine = counts[4, pl.ds(hi_own, 1), :]
    cnt[...] = jnp.broadcast_to(mine, (128, 256)).T
    rott[...] = rot[y].astype(F32).T

    def chunk(a, b):
        return pl.ds(pl.multiple_of(b * 1024 + a * OWN, OWN), OWN)

    def half_chunk(a, b, hb):
        return pl.ds(pl.multiple_of(b * 1024 + a * OWN + hb * 128, 128), 128)

    def quarter_chunk(a, b, hb, v):
        return pl.ds(pl.multiple_of(b * 1024 + a * OWN + hb * 128 + v * 64, 64), 64)

    def y_chunk_send(q, hb):
        ref = cent.at[half_chunk(zs_of[q], y, hb)]
        send("ca%d%d" % (q, hb), ref, ref, to_y(1))
        send("cb%d%d" % (q, hb), ref, ref, to_y(3))

    def y_chunk_forward(q, hb):
        a = zs_of[q]
        recv("ca%d%d" % (q, hb), cent.at[half_chunk(a, ym, hb)])
        ref = cent.at[quarter_chunk(a, ym, hb, 0)]
        send("cc%d%d" % (q, hb), ref, ref, to_y(1))
        recv("cb%d%d" % (q, hb), cent.at[half_chunk(a, yp, hb)])
        ref = cent.at[quarter_chunk(a, yp, hb, 1)]
        send("cd%d%d" % (q, hb), ref, ref, to_y(3))

    def z_chunk(q, hb):
        recv("cz%d%d" % (q, hb), cent.at[half_chunk(zs_of[q], y, hb)])
        y_chunk_send(q, hb)

    zs_of = [zh] + [lax.rem(zh + 4 - q, 4) for q in (1, 2, 3)]
    for hb in range(2):
        total = tacc[part(hb), pl.ds(pl.multiple_of(zh * DS, DS), DS)]
        for k in (1, 3, 2):
            recv("t%d%d" % (k, hb), trecv.at[k - 1, part(hb)])
            total = total + trecv[k - 1, part(hb), :].astype(F32)
        value = (total + cbk[part(hb), :].astype(F32)) / (cnt[part(hb), :] + 1.0)
        cent[half_chunk(zh, y, hb), :] = value.astype(BF16)
        ref = cent.at[half_chunk(zh, y, hb)]
        for k in (1, 3, 2):
            send("cz%d%d" % (k, hb), ref, ref, to_zh(k))
        y_chunk_send(0, hb)

    outs = []

    def rebuild(a, b):
        copy = pltpu.make_async_copy(
            cent.at[chunk(a, b)], cent_out.at[chunk(a, b)], lsem.at[5 + len(outs)]
        )
        copy.start()
        outs.append(copy)
        table = cent[chunk(a, b), :].astype(F32).T.astype(BF16)
        want = 4 * b + a
        for i in range(8):
            tab = lo[:, pl.ds(pl.multiple_of(y * GROUP + i * 256, 256), 256)]
            got = jnp.dot(table, tab, preferred_element_type=F32)
            place = slice(i * 256, (i + 1) * 256)
            row = jnp.concatenate([codes[y, i:i + 1, :], codes[y, i + 8:i + 9, :]], axis=1)
            hit = lax.shift_right_logical(row, 8) == want
            reb[:, place] = jnp.where(jnp.broadcast_to(hit, (128, 256)), got, reb[:, place])

    reb[...] = jnp.zeros_like(reb)
    vrecv("wp1", up_z, 1, core)
    vsend("w21", up_z, 1, core, to_xm)
    vsend("d_wp1", up_z, 1, core, to_core)
    vrecv("wm1", down_z, 1, core)
    vsend("d_wm1", down_z, 1, core, to_core)
    y_chunk_forward(0, 0)
    z_chunk(1, 0)
    z_chunk(3, 0)
    y_chunk_forward(0, 1)
    rebuild(zh, y)
    z_chunk(2, 0)
    y_chunk_forward(1, 0)
    y_chunk_forward(3, 0)
    rebuild(zh, ym)
    rebuild(zh, yp)
    z_chunk(1, 1)
    z_chunk(3, 1)
    y_chunk_forward(2, 0)
    z_chunk(2, 1)
    vrecv("w20", far_z, 0, core)
    vsend("d_w20", far_z, 0, core, to_core)
    vrecv("w21", far_z, 1, core)
    vsend("d_w21", far_z, 1, core, to_core)
    rebuild(zs_of[1], y)
    rebuild(zs_of[3], y)
    y_chunk_forward(1, 1)
    y_chunk_forward(3, 1)
    rebuild(zs_of[2], y)
    y_chunk_forward(2, 1)
    for q in (1, 3, 2):
        rebuild(zs_of[q], ym)
        rebuild(zs_of[q], yp)

    for q in (0, 1, 3, 2):
        a = zs_of[q]
        for hb in range(2):
            recv("cc%d%d" % (q, hb), cent.at[quarter_chunk(a, y2, hb, 0)])
            recv("cd%d%d" % (q, hb), cent.at[quarter_chunk(a, y2, hb, 1)])
        rebuild(a, y2)
    for h in range(2):
        vrecv("d_w%d" % h, here_z, h, co)
        vrecv("d_wm%d" % h, down_z, h, co)
        vrecv("d_wp%d" % h, up_z, h, co)
        vrecv("d_w2%d" % h, far_z, h, co)

    rebb[...] = reb[...].astype(BF16)

    pairs = ((2, 1), (3, 0))

    def cross_part(k, p):
        to = lax.rem(y + k, 4)
        blocks = []
        for z in pairs[p]:
            column = (lax.rem(zh + z, 4) * 4 + to) * 128
            blocks.append(vg[:, pl.ds(pl.multiple_of(column, 128), 128)])
        got = jnp.dot(rebb[...], jnp.concatenate(blocks, axis=1), preferred_element_type=F32)
        if k == 0:
            xf[p, 0] = got[:, :128]
            xf[p, 1] = got[:, 128:]
        else:
            xs[k - 1, p, 0] = got[:, :128].astype(BF16)
            xs[k - 1, p, 1] = got[:, 128:].astype(BF16)
            send("xa%d%d" % (k, p), xs.at[k - 1, p], xr.at[k - 1, p], to_y(k))

    for p in range(2):
        for k in (2, 1, 3):
            cross_part(k, p)
    for p in range(2):
        cross_part(0, p)

    gap = rott[...] - reb[...]
    gap = jnp.sum(gap * gap, axis=0, keepdims=True)
    half_row = lax.broadcasted_iota(jnp.int32, (1, 128), 1) < 64
    for cp in range(8):
        u0, u1 = gap[:, cp * 256:cp * 256 + 128], gap[:, cp * 256 + 128:cp * 256 + 256]
        dist_ref[2 * cp:2 * cp + 1, :] = jnp.where(half_row, u0, pltpu.roll(u1, 64, 1))
        dist_ref[2 * cp + 1:2 * cp + 2, :] = jnp.where(half_row, pltpu.roll(u0, 64, 1), u1)

    def cross_sum(p):
        for k in (1, 3, 2):
            recv("xa%d%d" % (k, p), xr.at[k - 1, p])
        return [xf[p, i] + xr[0, p, i].astype(F32) + xr[1, p, i].astype(F32) + xr[2, p, i].astype(F32) for i in range(2)]

    def cross_zh(k, value):
        zs[k - 1] = value.astype(BF16)
        send("xz%d" % k, zs.at[k - 1], zr.at[k - 1], to_zh(k))

    two, one = cross_sum(0)
    cross_zh(2, two)
    cross_zh(1, one)
    three, out = cross_sum(1)
    cross_zh(3, three)
    for k in (1, 2, 3):
        recv("xz%d" % k, zr.at[k - 1])
        out = out + zr[k - 1].astype(F32)
    cross_ref[...] = out.T

    for copy in outs:
        copy.wait()
    for copy in pending:
        copy.wait_send()


def hand_out(a_ref, b_ref, c_ref, a_out, b_out, c_out, sem):
    copies = [
        pltpu.make_async_copy(src, dst, sem.at[i])
        for i, (src, dst) in enumerate(((a_ref, a_out), (b_ref, b_out), (c_ref, c_out)))
    ]
    for copy in copies:
        copy.start()
    for copy in copies:
        copy.wait()


def per_device(vectors, rotation, codebook, codes):
    vmem = pl.BlockSpec(memory_space=pltpu.VMEM)
    hbm = pl.BlockSpec(memory_space=pltpu.HBM)
    operands = (vectors, rotation, codebook.reshape(K, DS), codes.reshape(16, 128))
    cent, dist, cross = pl.pallas_call(
        kernel,
        out_shape=(
            jax.ShapeDtypeStruct((K, DS), BF16),
            jax.ShapeDtypeStruct((16, 128), F32),
            jax.ShapeDtypeStruct((DS, DS), F32),
        ),
        in_specs=[hbm] * 4,
        out_specs=(pl.BlockSpec(memory_space=pl.ANY), vmem, vmem),
        scratch_shapes=[
            pltpu.VMEM((GROUP, D), BF16),
            pltpu.VMEM((4, GROUP, DS), BF16),
            pltpu.VMEM((GROUP, DS), BF16),
            pltpu.VMEM((DS, GROUP), F32),
            pltpu.VMEM((D, DS), BF16),
            pltpu.VMEM((D, DS), BF16),
            pltpu.VMEM((16, 128), jnp.int32),
            pltpu.VMEM((4, 16, 128), jnp.int32),
            pltpu.VMEM((256, 4 * GROUP), BF16),
            pltpu.VMEM((4, GROUP, DS), BF16),
            pltpu.VMEM((5, 16, 256), F32),
            pltpu.VMEM((256, 4 * DS), F32),
            pltpu.VMEM((3, OWN, DS), BF16),
            pltpu.VMEM((3, OWN, DS), BF16),
            pltpu.VMEM((OWN, DS), F32),
            pltpu.VMEM((OWN, DS), BF16),
            pltpu.VMEM((K, DS), BF16),
            pltpu.VMEM((DS, GROUP), F32),
            pltpu.VMEM((DS, GROUP), BF16),
            pltpu.VMEM((2, 2, DS, 128), F32),
            pltpu.VMEM((3, 2, 2, DS, 128), BF16),
            pltpu.VMEM((3, 2, 2, DS, 128), BF16),
            pltpu.VMEM((3, DS, 128), BF16),
            pltpu.VMEM((3, DS, 128), BF16),
            pltpu.SemaphoreType.DMA((SEMS,)),
            pltpu.SemaphoreType.DMA((SEMS,)),
            pltpu.SemaphoreType.DMA((21,)),
        ],
        compiler_params=pltpu.CompilerParams(
            collective_id=0, has_side_effects=True, vmem_limit_bytes=48 * 1024 * 1024
        ),
        name="opq_step",
    )(*(pltpu.with_memory_space_constraint(t, pltpu.HBM) for t in operands))
    whole = pl.BlockSpec(memory_space=pl.ANY)
    cent, dist, cross = pl.pallas_call(
        hand_out,
        out_shape=tuple(jax.ShapeDtypeStruct(t.shape, t.dtype) for t in (cent, dist, cross)),
        in_specs=[whole] * 3,
        out_specs=(whole,) * 3,
        scratch_shapes=[pltpu.SemaphoreType.DMA((3,))],
        compiler_params=pltpu.CompilerParams(vmem_limit_bytes=4 * 1024 * 1024),
        name="hand_out",
    )(cent, dist, cross)
    return cent.reshape(1, K, DS), dist.reshape(GROUP, 1), cross


def solution(mesh):
    placed = (P(("dp", "sub"), None), P(None, "sub"), P("sub", None, None), P("dp", "sub"))
    return jax.shard_map(
        per_device,
        mesh=mesh,
        in_specs=placed,
        out_specs=(P("sub", None, None), P("dp", "sub"), P("dp", "sub")),
        check_vma=False,
    )
```
